256 devices in a mesh: row: 16 (over z, core), col: 16 (over x, y).
Axes of the slice: x: 4, y: 4, z: 8, core: 2. Of those that a mesh axis runs over, the one named last changes fastest.
Arguments:
- rhs: float32 [16, 64, 128], P('col'), may hold values from -6 to 6
- diag_inv: float32 [16, 128, 128], P('col'), as said below
- panel: bfloat16 [16, 16, 128, 128], P('row', 'col'), may hold values from -0.09375 to 0.09375
- offdiag: bfloat16 [1024, 16, 128, 128], P('row', 'col'), may hold values from -0.015625 to 0.015625
- known: bfloat16 [512, 64, 128], P(('row', 'col')), may hold values from -6 to 6
- row_index: int32 [1024], P('row'), may hold values from 0 to 31
Outputs:
- solution: bfloat16 [16, 64, 128], P('col')
The draws below stay inside these ranges and needn't reach their ends.
Inputs may be any that keep to these rules, and one draw needn't show every extreme that they name: Each block of diag_inv is lower triangular (the inverse of a lower triangular diagonal block).
All inputs are finite; a program needn't handle non-finite values.
Results may differ from the reference program's by a relative error of at most 0.015.
Values may be sent and summed in bfloat16 or wider, within the bound.
A program may use at most 64 MiB of HBM per device.

```python
import jax
import jax.numpy as jnp
import numpy as np
from jax import lax

NB = 16
BS = 128
RHS = 64
OFF_DEV = 64
NOFF = 1024
K_ROW = 32
NK = 512
N_ROW = 16
N_COL = 16


def draw_diag_inv(key, part):
    first, second = jax.random.split(jax.random.fold_in(key, 17))
    lower = jnp.arange(BS)[:, None] > jnp.arange(BS)[None, :]
    eye = jnp.arange(BS)[:, None] == jnp.arange(BS)[None, :]
    spread = 0.5 * jax.random.normal(first, (NB, BS, BS), jnp.float32) / jnp.sqrt(jnp.float32(BS))
    diag = jax.random.uniform(second, (NB, BS, BS), jnp.float32, 0.6, 1.4)
    return jnp.where(lower[None], spread, 0.0) + jnp.where(eye[None], diag, 0.0)


def with_ends(values, own_key, low, top_value):
    spot = [jax.random.randint(jax.random.fold_in(own_key, axis), (), 0, length) for axis, length in enumerate(values.shape)]
    widest = values.shape.index(max(values.shape))
    beside = spot[:widest] + [(spot[widest] + 1) % values.shape[widest]] + spot[widest + 1:]
    return values.at[tuple(spot)].set(low).at[tuple(beside)].set(top_value)


def steps_of(own_key, shape, pieces, least, top_value):
    loudness = 1.0
    for axis_at, blocks in pieces:
        heights = jax.random.uniform(jax.random.fold_in(jax.random.fold_in(own_key, 6), axis_at), (blocks,), jnp.float32, least / len(pieces), top_value / len(pieces))
        loudness = loudness * jnp.repeat(jnp.exp(heights), shape[axis_at] // blocks).reshape((-1,) + (1,) * (len(shape) - 1 - axis_at))
    return loudness


def centred(stream_key, dims, width, limit, shards=(), dtype=jnp.bfloat16):
    values = jax.random.normal(stream_key, dims, jnp.float32) * width
    if len(shards) > 0:
        values = steps_of(stream_key, dims, shards, -0.22, 0.18) * values
    return jnp.clip(values, min=-limit, max=limit).astype(dtype)


def setup_inputs(seed: int = 0) -> dict:
    keys = jax.random.split(jax.random.key(seed), 7)
    rhs = centred(keys[0], (NB, RHS, BS), 1.0, 6.0, ((0, 16),), jnp.float32)
    diag_inv = draw_diag_inv(jax.random.fold_in(keys[6], 71), 0)
    panel = centred(keys[2], (NB, NB, BS, BS), (2 * NB * BS) ** -0.5, 0.09375, ((0, 16), (1, 16)))
    offdiag = centred(keys[3], (NOFF, NB, BS, BS), (NOFF * BS) ** -0.5, 0.015625, ((0, 16), (1, 16)))
    known = centred(keys[4], (NK, RHS, BS), 1.0, 6.0, ((0, 256),))
    row_index = with_ends(jax.random.randint(keys[5], (NOFF,), 0, K_ROW), jax.random.fold_in(keys[5], 1), 0, K_ROW - 1).astype(jnp.int32)
    return dict(rhs=rhs, diag_inv=diag_inv, panel=panel, offdiag=offdiag, known=known, row_index=row_index)


def positions(count, parts):
    return np.array([(k % parts) * (count // parts) + k // parts for k in range(count)])


def reference(rhs, diag_inv, panel, offdiag, known, row_index):
    col_pos = positions(NB, N_COL)
    row_pos = positions(NB, N_ROW)
    owner_base = jnp.asarray((np.arange(NOFF) // OFF_DEV) * K_ROW).astype(jnp.int32)
    picked = known[owner_base + row_index.astype(jnp.int32)].astype(jnp.float32)

    def one_column(stored):
        tiles = lax.dynamic_index_in_dim(offdiag, stored, 1, keepdims=False).astype(jnp.float32)
        return jnp.einsum('pqi,pia->qa', picked, tiles)

    off_sum = lax.map(one_column, jnp.asarray(col_pos).astype(jnp.int32))
    update = rhs[col_pos] - off_sum
    solved = [None] * NB
    for k in reversed(range(NB)):
        total = update[k]
        for j in range(k + 1, NB):
            total = total - jnp.dot(solved[j], panel[row_pos[j], col_pos[k]], preferred_element_type=jnp.float32)
        solved[k] = jnp.dot(total, diag_inv[col_pos[k]], precision=lax.Precision.HIGHEST, preferred_element_type=jnp.float32).astype(jnp.bfloat16)
    slots = NB // N_COL
    order = [(s % slots) * N_COL + s // slots for s in range(NB)]
    return jnp.stack([solved[k] for k in order])
```

```python
import functools

import jax
import jax.numpy as jnp
from jax import lax
from jax.experimental import pallas as pl
from jax.experimental.pallas import tpu as pltpu
from jax.sharding import PartitionSpec as P

NB = 16
BS = 128
RHS = 64
TILES = 64
NR = 16
NC = 16
NQ = 8
QR = RHS // NQ
CUT = 11
TRI = NB * (NB - 1) // 2
MESH = pl.DeviceIdType.MESH
BF = jnp.bfloat16
F32 = jnp.float32


def tri(j):
    return j * (j - 1) // 2


def split(value):
    high = value.astype(BF)
    return high, (value - high.astype(F32)).astype(BF)


def kernel(
    rhs_hbm, dinv_hbm, panel_hbm, offdiag_hbm, known_hbm, row_index, out_ref,
    rhs_v, dinv_v, panel_v, off_v, known_v, scaled_v, part_v, pieces_v, panels_v,
    mine_v, pass_v, passed_v, blocks_v,
    load_sem, off_sem, all_in, known_send, known_recv, panel_send, panel_recv,
    part_send, part_recv, pass_send, pass_recv, block_send, block_recv,
):
    r = lax.axis_index("row")
    c = lax.axis_index("col")

    def remote(src, dst, send, recv, row, col):
        return pltpu.make_async_remote_copy(
            src_ref=src, dst_ref=dst, send_sem=send, recv_sem=recv,
            device_id=(row, col), device_id_type=MESH,
        )

    def solver(high, q):
        return 2 * q, jnp.where(high, NC - 4, 0) + q % 4

    barrier = pltpu.get_barrier_semaphore()
    for d in range(1, NC):
        pl.semaphore_signal(barrier, inc=1, device_id=(r, (c + d) % NC), device_id_type=MESH)
    for d in range(1, NR):
        pl.semaphore_signal(barrier, inc=1, device_id=((r + d) % NR, c), device_id_type=MESH)

    mine = pl.ds(2 * c, 2)
    loads = [
        pltpu.make_async_copy(known_hbm, known_v.at[mine], load_sem.at[0]),
        pltpu.make_async_copy(dinv_hbm.at[0], dinv_v, load_sem.at[1]),
        pltpu.make_async_copy(panel_hbm.at[0, 0], panel_v, load_sem.at[2]),
        pltpu.make_async_copy(rhs_hbm.at[0], rhs_v, load_sem.at[3]),
    ]
    for load in loads:
        load.start()
    off_load = pltpu.make_async_copy(offdiag_hbm.at[:, 0], off_v, off_sem)
    off_load.start()
    for load in loads:
        load.wait()

    d_high, d_low = split(dinv_v[...])
    block = panel_v[...]
    scaled = jnp.dot(
        jnp.concatenate([block, block], axis=1),
        jnp.concatenate([d_high, d_low], axis=0),
        preferred_element_type=F32,
    )
    scaled_v[...] = (-scaled).astype(BF)

    pl.semaphore_wait(barrier, NC - 1 + NR - 1)

    for d in (5, 15, 7, 13, 10, 9, 6, 14, 11, 2, 8, 1, 4, 3, 12):
        peer = ((c // 4 + d // 4) % 4) * 4 + (c + d) % 4
        remote(known_v.at[mine], known_v.at[mine], known_send, known_recv, r, peer).start()

    for d in range(1, NR):
        pl.semaphore_signal(all_in, inc=1, device_id=((r + d) % NR, c), device_id_type=MESH)
    pl.semaphore_wait(all_in, NR - 1)

    def panel_copy(q, which):
        row, col = solver(r >= CUT, (r // 2 + q) % NQ)
        spot = tri(r) + c
        if which == "local":
            return pltpu.make_async_copy(scaled_v, panels_v.at[spot], panel_recv.at[r])
        return remote(scaled_v, panels_v.at[spot], panel_send, panel_recv.at[r], row, col)

    own_col = jnp.where(r >= CUT, NC - 4, 0) + (r // 2) % 4
    panel_self = (r % 2 == 0) & (c == own_col)

    @pl.when(c < r)
    def _():
        for q in range(NQ):
            if q == 0:
                pl.when(panel_self)(lambda: panel_copy(0, "local").start())
                pl.when(jnp.logical_not(panel_self))(lambda: panel_copy(0, "remote").start())
            else:
                panel_copy(q, "remote").start()

    rest = pl.ds(0, 2 * (NC - 1))
    remote(known_v.at[rest], known_v.at[rest], known_send, known_recv, r, (c + 1) % NC).wait_recv()
    off_load.wait()
    total = jnp.zeros((RHS, BS), F32)
    for p in range(0, TILES, 2):
        picked = jnp.concatenate([known_v[row_index[p]], known_v[row_index[p + 1]]], axis=1)
        total = total + jnp.dot(
            picked, off_v[p : p + 2].reshape(2 * BS, BS), preferred_element_type=F32
        )
    once = (r == 0).astype(F32)
    t_high, t_low = split(rhs_v[...] * once - total)
    part = jnp.dot(
        jnp.concatenate([t_high, t_high, t_low], axis=1),
        jnp.concatenate([d_high, d_low, d_high], axis=0),
        preferred_element_type=F32,
    )
    part_v[...] = part.astype(BF).reshape(NQ, QR, BS)

    part_col = jnp.where(c >= CUT, NC - 4, 0) + (r // 2) % 4
    part_self = (r % 2 == 0) & (c == part_col)

    def part_copy(q, which):
        group = (r // 2 + q) % NQ
        row, col = solver(c >= CUT, group)
        if which == "local":
            return pltpu.make_async_copy(part_v.at[group], pieces_v.at[c, r], part_recv.at[c])
        return remote(part_v.at[group], pieces_v.at[c, r], part_send, part_recv.at[c], row, col)

    for q in range(NQ):
        if q == 0:
            pl.when(part_self)(lambda: part_copy(0, "local").start())
            pl.when(jnp.logical_not(part_self))(lambda: part_copy(0, "remote").start())
        else:
            part_copy(q, "remote").start()

    my_q = r // 2
    even = r % 2 == 0
    is_high = even & (c == NC - 4 + my_q % 4)
    is_low = even & (c == my_q % 4)

    def block_copy(k, d, which):
        if which == "local":
            return pltpu.make_async_copy(mine_v.at[k], blocks_v.at[my_q], block_recv)
        row = (r + d) % NR
        return remote(mine_v.at[k], blocks_v.at[my_q], block_send.at[k], block_recv, row, k)

    def send_block(k):
        for d in range(NR):
            if d == 0:
                pl.when(c == k)(lambda: block_copy(k, 0, "local").start())
                pl.when(c != k)(lambda: block_copy(k, 0, "remote").start())
            else:
                block_copy(k, d, "remote").start()

    def finish_block(k):
        for d in range(NR):
            if d == 0:
                pl.when(c != k)(lambda: block_copy(k, 0, "remote").wait_send())
            else:
                block_copy(k, d, "remote").wait_send()

    def summed(k):
        pltpu.make_async_copy(pieces_v.at[k], pieces_v.at[k], part_recv.at[k]).wait()
        return jnp.sum(pieces_v[k].astype(F32), axis=0)

    def rows_in(j):
        if j > 0:
            spots = pl.ds(tri(j), j)
            pltpu.make_async_copy(panels_v.at[spots], panels_v.at[spots], panel_recv.at[j]).wait()

    def eliminate(j, sums):
        done = sums[j].astype(BF)
        mine_v[j] = done
        send_block(j)
        for k in range(j - 1, -1, -1):
            term = jnp.dot(done, panels_v[tri(j) + k], preferred_element_type=F32)
            sums[k] = term if sums[k] is None else sums[k] + term

    @pl.when(is_high)
    def _():
        for j in range(NB - 1, CUT - 1, -1):
            rows_in(j)
        sums = [None] * CUT + [summed(k) for k in range(CUT, NB)]
        for j in range(NB - 1, CUT - 1, -1):
            eliminate(j, sums)
        for k in range(CUT):
            pass_v[k] = sums[k]
        remote(pass_v, passed_v, pass_send, pass_recv, r, my_q % 4).start()
        remote(pass_v, passed_v, pass_send, pass_recv, r, my_q % 4).wait_send()
        for k in range(CUT, NB):
            finish_block(k)

    @pl.when(is_low)
    def _():
        for j in range(CUT - 1, -1, -1):
            rows_in(j)
        sums = [summed(k) for k in range(CUT)]
        remote(pass_v, passed_v, pass_send, pass_recv, r, my_q % 4 + NC - 4).wait_recv()
        sums = [sums[k] + passed_v[k] for k in range(CUT)]
        for j in range(CUT - 1, -1, -1):
            eliminate(j, sums)
        for k in range(CUT):
            finish_block(k)

    pltpu.make_async_copy(blocks_v, blocks_v, block_recv).wait()
    out_ref[0] = blocks_v[...].reshape(RHS, BS)

    remote(known_v.at[rest], known_v.at[rest], known_send, known_recv, r, (c + 1) % NC).wait_send()

    @pl.when(c < r)
    def _():
        pl.when(jnp.logical_not(panel_self))(lambda: panel_copy(0, "remote").wait_send())
        for q in range(1, NQ):
            panel_copy(q, "remote").wait_send()

    pl.when(jnp.logical_not(part_self))(lambda: part_copy(0, "remote").wait_send())
    for q in range(1, NQ):
        part_copy(q, "remote").wait_send()


def body(rhs, diag_inv, panel, offdiag, known, row_index):
    anywhere = pl.BlockSpec(memory_space=pl.ANY)
    dma = pltpu.SemaphoreType.DMA
    return pl.pallas_call(
        kernel,
        out_shape=jax.ShapeDtypeStruct((1, RHS, BS), BF),
        in_specs=[anywhere] * 5 + [pl.BlockSpec(memory_space=pltpu.SMEM)],
        out_specs=pl.BlockSpec(memory_space=pltpu.VMEM),
        scratch_shapes=[
            pltpu.VMEM((RHS, BS), F32),
            pltpu.VMEM((BS, BS), F32),
            pltpu.VMEM((BS, BS), BF),
            pltpu.VMEM((TILES, BS, BS), BF),
            pltpu.VMEM((2 * NC, RHS, BS), BF),
            pltpu.VMEM((BS, BS), BF),
            pltpu.VMEM((NQ, QR, BS), BF),
            pltpu.VMEM((NC, NR, QR, BS), BF),
            pltpu.VMEM((TRI, BS, BS), BF),
            pltpu.VMEM((NB, QR, BS), BF),
            pltpu.VMEM((CUT, QR, BS), F32),
            pltpu.VMEM((CUT, QR, BS), F32),
            pltpu.VMEM((NQ, QR, BS), BF),
            dma((4,)),
            dma,
            pltpu.SemaphoreType.REGULAR,
            dma, dma, dma, dma((NR,)), dma, dma((NC,)), dma, dma, dma((NB,)), dma,
        ],
        compiler_params=pltpu.CompilerParams(
            collective_id=0, has_side_effects=True, vmem_limit_bytes=32 << 20
        ),
    )(rhs, diag_inv, panel, offdiag, known, row_index)


def solution(mesh):
    placed = (
        P("col", None, None),
        P("col", None, None),
        P("row", "col", None, None),
        P("row", "col", None, None),
        P(("row", "col"), None, None),
        P("row"),
    )
    return jax.shard_map(
        body, mesh=mesh, in_specs=placed, out_specs=P("col", None, None), check_vma=False
    )
```

```python
import jax
import jax.numpy as jnp
from jax import lax
from jax.experimental import pallas as pl
from jax.experimental.pallas import tpu as pltpu
from jax.sharding import PartitionSpec as P

NB = 16
BS = 128
RHS = 64
TILES = 64
NR = 16
NC = 16
NQ = 4
QR = RHS // NQ
CUT = 11
TOP = NB - CUT
SIDE = 4
MESH = pl.DeviceIdType.MESH
BF = jnp.bfloat16
F32 = jnp.float32
SPOT_Z = (0, 1, 2, 3)
HIGH_X = (3, 2) * 4
LOW_X = (0, 1) * 4


def tri(j):
    return j * (j - 1) // 2


def spot(j, k):
    d = k - CUT
    return d * (TOP - 1) - d * (d - 1) // 2 + j - k - 1


def split(value):
    high = value.astype(BF)
    return high, (value - high.astype(F32)).astype(BF)


def kernel(
    rhs_hbm, dinv_hbm, panel_hbm, offdiag_hbm, known_hbm, row_index, out_ref,
    rhs_v, dinv_v, panel_v, off_v, known_v, scaled_v, part_v, pieces_v,
    top_v, cross_v, low_v, mine_v, pass_v, passed_v, blocks_v,
    load_sem, off_sem, planes_in, all_in, known_send, known_recv,
    panel_send, top_recv, cross_recv, low_recv, share_send, share_recv,
    part_send, part_recv, pass_send, pass_recv, block_send, block_recv,
):
    r = lax.axis_index("row")
    c = lax.axis_index("col")
    y = c % SIDE

    def signal(sem, row, col):
        pl.semaphore_signal(sem, inc=1, device_id=(row, col), device_id_type=MESH)

    def remote(src, dst, send, recv, row, col):
        return pltpu.make_async_remote_copy(
            src_ref=src, dst_ref=dst, send_sem=send, recv_sem=recv,
            device_id=(row, col), device_id_type=MESH,
        )

    def start_to(place, src, dst, send, recv):
        here = (r == place[0]) & (c == place[1])
        pl.when(here)(lambda: pltpu.make_async_copy(src, dst, recv).start())
        pl.when(jnp.logical_not(here))(lambda: remote(src, dst, send, recv, *place).start())

    def finish_to(place, src, send, recv):
        here = (r == place[0]) & (c == place[1])
        pl.when(jnp.logical_not(here))(lambda: remote(src, src, send, recv, *place).wait_send())

    def arrived(dst, sem):
        pltpu.make_async_copy(dst, dst, sem).wait()

    def high_at(q, i):
        return 2 * SPOT_Z[q], HIGH_X[q] * SIDE + i

    def low_at(q):
        return 2 * SPOT_Z[q], LOW_X[q] * SIDE

    barrier = pltpu.get_barrier_semaphore()
    for d in range(1, NC):
        signal(barrier, r, (c + d) % NC)

    @pl.when(c == 0)
    def _():
        for d in range(1, NR):
            signal(barrier, (r + d) % NR, 0)

    mine = pl.ds(2 * c, 2)
    known_load = pltpu.make_async_copy(known_hbm, known_v.at[mine], load_sem.at[0])
    loads = [
        pltpu.make_async_copy(dinv_hbm.at[0], dinv_v, load_sem.at[1]),
        pltpu.make_async_copy(panel_hbm.at[0, 0], panel_v, load_sem.at[2]),
        pltpu.make_async_copy(rhs_hbm.at[0], rhs_v, load_sem.at[3]),
    ]
    known_load.start()
    for load in loads:
        load.start()
    off_load = pltpu.make_async_copy(offdiag_hbm.at[:, 0], off_v, off_sem)
    off_load.start()
    known_load.wait()
    pl.when(c == 0)(lambda: pl.semaphore_wait(barrier, NC - 1 + NR - 1))
    pl.when(c != 0)(lambda: pl.semaphore_wait(barrier, NC - 1))

    for d in (5, 15, 7, 13, 10, 9, 6, 14, 11, 2, 8, 1, 4, 3, 12):
        peer = ((c // SIDE + d // SIDE) % SIDE) * SIDE + (c + d) % SIDE
        remote(known_v.at[mine], known_v.at[mine], known_send, known_recv, r, peer).start()

    @pl.when(c == 0)
    def _():
        for d in range(1, NR):
            signal(planes_in, (r + d) % NR, 0)

    for load in loads:
        load.wait()
    d_high, d_low = split(dinv_v[...])
    block = panel_v[...]
    scaled = jnp.dot(
        jnp.concatenate([block, block], axis=1),
        jnp.concatenate([d_high, d_low], axis=0),
        preferred_element_type=F32,
    )
    scaled_v[...] = (-scaled).astype(BF)

    @pl.when(c == 0)
    def _():
        pl.semaphore_wait(planes_in, NR - 1)
        for d in range(1, NC):
            signal(all_in, r, (c + d) % NC)

    @pl.when(c != 0)
    def _():
        pl.semaphore_wait(all_in, 1)

    in_top = (r >= CUT) & (c >= CUT) & (c < r)
    in_cross = (r >= CUT) & (c < CUT)
    in_low = (r < CUT) & (c < r)

    @pl.when(in_top)
    def _():
        for q in range(NQ):
            start_to(high_at(q, y), scaled_v, top_v.at[spot(r, c)], panel_send, top_recv)

    @pl.when(in_cross)
    def _():
        for q in range(NQ):
            start_to(high_at(q, y), scaled_v, cross_v.at[c // SIDE, NB - 1 - r], panel_send, cross_recv)

    @pl.when(in_low)
    def _():
        for q in range(NQ):
            start_to(low_at(q), scaled_v, low_v.at[tri(r) + c], panel_send, low_recv)

    rest = pl.ds(0, 2 * (NC - 1))
    arrived(known_v.at[rest], known_recv)
    off_load.wait()
    total = jnp.zeros((RHS, BS), F32)
    for p in range(0, TILES, 2):
        picked = jnp.concatenate([known_v[row_index[p]], known_v[row_index[p + 1]]], axis=1)
        total = total + jnp.dot(
            picked, off_v[p : p + 2].reshape(2 * BS, BS), preferred_element_type=F32
        )
    once = (r == 0).astype(F32)
    t_high, t_low = split(rhs_v[...] * once - total)
    part = jnp.dot(
        jnp.concatenate([t_high, t_high, t_low], axis=1),
        jnp.concatenate([d_high, d_low, d_high], axis=0),
        preferred_element_type=F32,
    )
    part_v[...] = part.astype(BF).reshape(NQ, QR, BS)

    @pl.when(c >= CUT)
    def _():
        for q in range(NQ):
            for i in range(SIDE):
                start_to(high_at(q, i), part_v.at[q], pieces_v.at[c, r], part_send, part_recv)

    @pl.when(c < CUT)
    def _():
        for q in range(NQ):
            start_to(low_at(q), part_v.at[q], pieces_v.at[c, r], part_send, part_recv)

    def block_copy(k, d, my_q):
        return remote(
            mine_v.at[k], blocks_v.at[my_q], block_send.at[k], block_recv, (r + d) % NR, k
        )

    def send_block(k, my_q, may_be_own):
        for d in range(NR):
            if d == 0 and may_be_own:
                own = pltpu.make_async_copy(mine_v.at[k], blocks_v.at[my_q], block_recv)
                pl.when(c == k)(lambda: own.start())
                pl.when(c != k)(lambda: block_copy(k, 0, my_q).start())
            else:
                block_copy(k, d, my_q).start()

    def finish_block(k, my_q, may_be_own):
        for d in range(NR):
            if d == 0 and may_be_own:
                pl.when(c != k)(lambda: block_copy(k, 0, my_q).wait_send())
            else:
                block_copy(k, d, my_q).wait_send()

    def member(places):
        one, which = jnp.bool_(False), jnp.int32(0)
        for q, options in enumerate(places):
            here = jnp.bool_(False)
            for row, col in options:
                here = here | ((r == row) & (c == col))
            one, which = one | here, which + jnp.where(here, q, 0)
        return one, which

    is_high, high_q = member([[high_at(q, i) for i in range(SIDE)] for q in range(NQ)])
    is_low, low_q = member([[low_at(q)] for q in range(NQ)])

    def summed(k):
        return jnp.sum(pieces_v[k].astype(F32), axis=0)

    @pl.when(is_high)
    def _():
        for k in range(CUT, NB - 1):
            count = NB - 1 - k
            column = top_v.at[pl.ds(spot(k + 1, k), count)]
            others = top_v.at[pl.ds(0, tri(TOP) - count)]

            def to(d):
                return remote(column, column, share_send, share_recv, r, c - y + (y + d) % SIDE)

            @pl.when(y == k % SIDE)
            def _():
                arrived(column, top_recv)
                for d in range(1, SIDE):
                    to(d).start()
                arrived(others, share_recv)
                for d in range(1, SIDE):
                    to(d).wait_send()

        pl.when(y < CUT - 2 * SIDE)(lambda: arrived(cross_v, cross_recv))
        pl.when(y >= CUT - 2 * SIDE)(lambda: arrived(cross_v.at[pl.ds(0, 2)], cross_recv))
        arrived(pieces_v.at[pl.ds(CUT, TOP)], part_recv)
        sums = [summed(k) for k in range(CUT, NB)]
        done = [None] * TOP
        for j in range(TOP - 1, -1, -1):
            done[j] = sums[j].astype(BF)
            mine_v[CUT + j] = done[j]
            for k in range(j - 1, -1, -1):
                sums[k] += jnp.dot(done[j], top_v[spot(CUT + j, CUT + k)], preferred_element_type=F32)
        joined = jnp.concatenate(done[::-1], axis=1)
        low_col = (SIDE - 1 - c // SIDE) * SIDE

        def cross(t):
            return remote(
                pass_v.at[t], passed_v.at[t * SIDE + y], pass_send, pass_recv, r, low_col
            )

        def send_cross(t):
            pass_v[t] = jnp.dot(
                joined, cross_v[t].reshape(TOP * BS, BS), preferred_element_type=F32
            )
            cross(t).start()

        @pl.when(y < CUT - 2 * SIDE)
        def _():
            send_cross(2)

        send_cross(1)
        send_cross(0)
        for k in range(CUT, NB):
            pl.when(y == k % SIDE)(lambda: send_block(k, high_q, True))
        cross(0).wait_send()
        cross(1).wait_send()
        pl.when(y < CUT - 2 * SIDE)(lambda: cross(2).wait_send())
        for k in range(CUT, NB):
            pl.when(y == k % SIDE)(lambda: finish_block(k, high_q, True))

    @pl.when(is_low)
    def _():
        arrived(low_v, low_recv)
        arrived(pieces_v.at[pl.ds(0, CUT)], part_recv)
        sums = [summed(k) for k in range(CUT)]
        arrived(passed_v, pass_recv)
        sums = [sums[k] + passed_v[k] for k in range(CUT)]
        for j in range(CUT - 1, -1, -1):
            done = sums[j].astype(BF)
            mine_v[j] = done
            send_block(j, low_q, j in (0, SIDE))
            for k in range(j - 1, -1, -1):
                sums[k] += jnp.dot(done, low_v[tri(j) + k], preferred_element_type=F32)
        for k in range(CUT):
            finish_block(k, low_q, k in (0, SIDE))

    arrived(blocks_v, block_recv)
    out_ref[0] = blocks_v[...].reshape(RHS, BS)

    remote(known_v.at[rest], known_v.at[rest], known_send, known_recv, r, (c + 1) % NC).wait_send()

    @pl.when(in_top)
    def _():
        for q in range(NQ):
            finish_to(high_at(q, y), scaled_v, panel_send, top_recv)

    @pl.when(in_cross)
    def _():
        for q in range(NQ):
            finish_to(high_at(q, y), scaled_v, panel_send, cross_recv)

    @pl.when(in_low)
    def _():
        for q in range(NQ):
            finish_to(low_at(q), scaled_v, panel_send, low_recv)

    @pl.when(c >= CUT)
    def _():
        for q in range(NQ):
            for i in range(SIDE):
                finish_to(high_at(q, i), part_v.at[q], part_send, part_recv)

    @pl.when(c < CUT)
    def _():
        for q in range(NQ):
            finish_to(low_at(q), part_v.at[q], part_send, part_recv)


def body(rhs, diag_inv, panel, offdiag, known, row_index):
    anywhere = pl.BlockSpec(memory_space=pl.ANY)
    dma = pltpu.SemaphoreType.DMA
    regular = pltpu.SemaphoreType.REGULAR
    return pl.pallas_call(
        kernel,
        out_shape=jax.ShapeDtypeStruct((1, RHS, BS), BF),
        in_specs=[anywhere] * 5 + [pl.BlockSpec(memory_space=pltpu.SMEM)],
        out_specs=pl.BlockSpec(memory_space=pltpu.VMEM),
        scratch_shapes=[
            pltpu.VMEM((RHS, BS), F32),
            pltpu.VMEM((BS, BS), F32),
            pltpu.VMEM((BS, BS), BF),
            pltpu.VMEM((TILES, BS, BS), BF),
            pltpu.VMEM((2 * NC, RHS, BS), BF),
            pltpu.VMEM((BS, BS), BF),
            pltpu.VMEM((NQ, QR, BS), BF),
            pltpu.VMEM((NC, NR, QR, BS), BF),
            pltpu.VMEM((tri(TOP), BS, BS), BF),
            pltpu.VMEM((3, TOP, BS, BS), BF),
            pltpu.VMEM((tri(CUT), BS, BS), BF),
            pltpu.VMEM((NB, QR, BS), BF),
            pltpu.VMEM((3, QR, BS), F32),
            pltpu.VMEM((CUT, QR, BS), F32),
            pltpu.VMEM((NQ, QR, BS), BF),
            dma((4,)), dma, regular, regular, dma, dma,
            dma, dma, dma, dma, dma, dma,
            dma, dma, dma, dma, dma((NB,)), dma,
        ],
        compiler_params=pltpu.CompilerParams(collective_id=0, has_side_effects=True),
    )(rhs, diag_inv, panel, offdiag, known, row_index)


def solution(mesh):
    placed = (
        P("col", None, None),
        P("col", None, None),
        P("row", "col", None, None),
        P("row", "col", None, None),
        P(("row", "col"), None, None),
        P("row"),
    )
    return jax.shard_map(
        body, mesh=mesh, in_specs=placed, out_specs=P("col", None, None), check_vma=False
    )
```

```python
import jax
import jax.numpy as jnp
from jax import lax
from jax.experimental import pallas as pl
from jax.experimental.pallas import tpu as pltpu
from jax.sharding import PartitionSpec as P

NB = 16
BS = 128
RHS = 64
TILES = 64
NR = 16
NC = 16
NQ = 4
QR = RHS // NQ
NL = 8
LR = RHS // NL
PER = NL // NQ
CUT = 11
TOP = NB - CUT
SIDE = 4
MESH = pl.DeviceIdType.MESH
BF = jnp.bfloat16
F32 = jnp.float32
SPOT_Z = (0, 1, 2, 3)
HIGH_X = (3, 3, 3, 3)
LOW_X = (0, 1)


def tri(j):
    return j * (j - 1) // 2


def spot(j, k):
    d = k - CUT
    return d * (TOP - 1) - d * (d - 1) // 2 + j - k - 1


def split(value):
    high = value.astype(BF)
    return high, (value - high.astype(F32)).astype(BF)


def kernel(
    rhs_hbm, dinv_hbm, panel_hbm, offdiag_hbm, known_hbm, row_index, out_ref,
    rhs_v, dinv_v, panel_v, off_v, known_v, scaled_v,
    high_part_v, low_part_v, high_pieces_v, low_pieces_v, top_v, cross_v, low_v,
    high_mine_v, low_mine_v, pass_v, passed_v, high_blocks_v, low_blocks_v,
    load_sem, off_sem, planes_in, all_in, known_send, known_recv,
    panel_send, top_recv, cross_recv, low_recv, share_send, share_recv,
    part_send, part_recv, pass_send, pass_recv, block_send, block_recv,
):
    r = lax.axis_index("row")
    c = lax.axis_index("col")
    y = c % SIDE

    def signal(sem, row, col):
        pl.semaphore_signal(sem, inc=1, device_id=(row, col), device_id_type=MESH)

    def remote(src, dst, send, recv, row, col):
        return pltpu.make_async_remote_copy(
            src_ref=src, dst_ref=dst, send_sem=send, recv_sem=recv,
            device_id=(row, col), device_id_type=MESH,
        )

    def start_to(place, src, dst, send, recv):
        here = (r == place[0]) & (c == place[1])
        pl.when(here)(lambda: pltpu.make_async_copy(src, dst, recv).start())
        pl.when(jnp.logical_not(here))(lambda: remote(src, dst, send, recv, *place).start())

    def finish_to(place, src, send, recv):
        here = (r == place[0]) & (c == place[1])
        pl.when(jnp.logical_not(here))(lambda: remote(src, src, send, recv, *place).wait_send())

    def arrived(dst, sem):
        pltpu.make_async_copy(dst, dst, sem).wait()

    def high_at(q, i):
        return 2 * SPOT_Z[q], HIGH_X[q] * SIDE + i

    def low_at(g):
        return 2 * SPOT_Z[g // PER], LOW_X[g % PER] * SIDE

    def member(places):
        one, which = jnp.bool_(False), jnp.int32(0)
        for q, options in enumerate(places):
            here = jnp.bool_(False)
            for row, col in options:
                here = here | ((r == row) & (c == col))
            one, which = one | here, which + jnp.where(here, q, 0)
        return one, which

    is_high, high_q = member([[high_at(q, i) for i in range(SIDE)] for q in range(NQ)])
    is_low, low_q = member([[low_at(g)] for g in range(NL)])

    barrier = pltpu.get_barrier_semaphore()
    for d in range(1, NC):
        signal(barrier, r, (c + d) % NC)

    @pl.when(c == 0)
    def _():
        for d in range(1, NR):
            signal(barrier, (r + d) % NR, 0)

    @pl.when(is_high)
    def _():
        for j in range(CUT, NB):
            for t in range(SIDE):
                pl.when(t * SIDE + y < j)(lambda: signal(barrier, j, t * SIDE + y))

    @pl.when(is_low)
    def _():
        for j in range(1, CUT):
            for k in range(j):
                if k % SIDE == 0:
                    pl.when((r != j) | (c != k))(lambda: signal(barrier, j, k))
                else:
                    signal(barrier, j, k)

    mine = pl.ds(2 * c, 2)
    known_load = pltpu.make_async_copy(known_hbm, known_v.at[mine], load_sem.at[0])
    loads = [
        pltpu.make_async_copy(dinv_hbm.at[0], dinv_v, load_sem.at[1]),
        pltpu.make_async_copy(panel_hbm.at[0, 0], panel_v, load_sem.at[2]),
        pltpu.make_async_copy(rhs_hbm.at[0], rhs_v, load_sem.at[3]),
    ]
    known_load.start()
    for load in loads:
        load.start()
    off_load = pltpu.make_async_copy(offdiag_hbm.at[:, 0], off_v, off_sem)
    off_load.start()
    known_load.wait()
    greeted = NC - 1 + jnp.where(c == 0, NR - 1, 0) + jnp.where(c < r, jnp.where(r < CUT, NL, NQ), 0)
    pl.semaphore_wait(barrier, greeted - jnp.where(is_low & (c < r), 1, 0))

    for d in (5, 15, 7, 13, 10, 9, 6, 14, 11, 2, 8, 1, 4, 3, 12):
        peer = ((c // SIDE + d // SIDE) % SIDE) * SIDE + (c + d) % SIDE
        remote(known_v.at[mine], known_v.at[mine], known_send, known_recv, r, peer).start()

    @pl.when(c == 0)
    def _():
        for d in range(1, NR):
            signal(planes_in, (r + d) % NR, 0)

    for load in loads:
        load.wait()
    d_high, d_low = split(dinv_v[...])
    block = panel_v[...]
    scaled = jnp.dot(
        jnp.concatenate([block, block], axis=1),
        jnp.concatenate([d_high, d_low], axis=0),
        preferred_element_type=F32,
    )
    scaled_v[...] = (-scaled).astype(BF)

    in_top = (r >= CUT) & (c >= CUT) & (c < r)
    in_cross = (r >= CUT) & (c < CUT)
    in_low = (r < CUT) & (c < r)

    @pl.when(in_top)
    def _():
        for q in range(NQ):
            start_to(high_at(q, y), scaled_v, top_v.at[spot(r, c)], panel_send, top_recv)

    @pl.when(in_cross)
    def _():
        for q in range(NQ):
            start_to(high_at(q, y), scaled_v, cross_v.at[c // SIDE, NB - 1 - r], panel_send, cross_recv)

    @pl.when(in_low)
    def _():
        for q in range(NL):
            start_to(low_at(q), scaled_v, low_v.at[tri(r) + c], panel_send, low_recv)

    @pl.when(c == 0)
    def _():
        pl.semaphore_wait(planes_in, NR - 1)
        for d in range(1, NC):
            signal(all_in, r, (c + d) % NC)

    @pl.when(c != 0)
    def _():
        pl.semaphore_wait(all_in, 1)

    rest = pl.ds(0, 2 * (NC - 1))
    arrived(known_v.at[rest], known_recv)
    off_load.wait()
    total = jnp.zeros((RHS, BS), F32)
    for p in range(0, TILES, 2):
        picked = jnp.concatenate([known_v[row_index[p]], known_v[row_index[p + 1]]], axis=1)
        total = total + jnp.dot(
            picked, off_v[p : p + 2].reshape(2 * BS, BS), preferred_element_type=F32
        )
    once = (r == 0).astype(F32)
    t_high, t_low = split(rhs_v[...] * once - total)
    part = jnp.dot(
        jnp.concatenate([t_high, t_high, t_low], axis=1),
        jnp.concatenate([d_high, d_low, d_high], axis=0),
        preferred_element_type=F32,
    )
    part = part.astype(BF)
    high_part_v[...] = part.reshape(NQ, QR, BS)
    low_part_v[...] = part.reshape(NL, LR, BS)

    @pl.when(c >= CUT)
    def _():
        for q in range(NQ):
            for i in range(SIDE):
                start_to(high_at(q, i), high_part_v.at[q], high_pieces_v.at[c - CUT, r], part_send, part_recv)

    @pl.when(c < CUT)
    def _():
        for q in range(NL):
            start_to(low_at(q), low_part_v.at[q], low_pieces_v.at[c, r], part_send, part_recv)

    def block_copy(k, d, block, slot):
        return remote(block, slot, block_send.at[k], block_recv, (r + d) % NR, k)

    def send_block(k, block, slot, may_be_own):
        for d in range(NR):
            if d == 0 and may_be_own:
                own = pltpu.make_async_copy(block, slot, block_recv)
                pl.when(c == k)(lambda: own.start())
                pl.when(c != k)(lambda: block_copy(k, 0, block, slot).start())
            else:
                block_copy(k, d, block, slot).start()

    def finish_block(k, block, slot, may_be_own):
        for d in range(NR):
            if d == 0 and may_be_own:
                pl.when(c != k)(lambda: block_copy(k, 0, block, slot).wait_send())
            else:
                block_copy(k, d, block, slot).wait_send()

    def summed(pieces):
        return jnp.sum(pieces.astype(F32), axis=0)

    @pl.when(is_high)
    def _():
        for k in range(CUT, NB - 1):
            count = NB - 1 - k
            column = top_v.at[pl.ds(spot(k + 1, k), count)]
            others = top_v.at[pl.ds(0, tri(TOP) - count)]

            def to(d):
                return remote(column, column, share_send, share_recv, r, c - y + (y + d) % SIDE)

            @pl.when(y == k % SIDE)
            def _():
                arrived(column, top_recv)
                for d in range(1, SIDE):
                    to(d).start()
                arrived(others, share_recv)
                for d in range(1, SIDE):
                    to(d).wait_send()

        pl.when(y < CUT - 2 * SIDE)(lambda: arrived(cross_v, cross_recv))
        pl.when(y >= CUT - 2 * SIDE)(lambda: arrived(cross_v.at[pl.ds(0, 2)], cross_recv))
        arrived(high_pieces_v, part_recv)
        sums = [summed(high_pieces_v[k]) for k in range(TOP)]
        done = [None] * TOP
        for j in range(TOP - 1, -1, -1):
            done[j] = sums[j].astype(BF)
            high_mine_v[j] = done[j]
            for k in range(j - 1, -1, -1):
                sums[k] += jnp.dot(done[j], top_v[spot(CUT + j, CUT + k)], preferred_element_type=F32)
        joined = jnp.concatenate(done[::-1], axis=1)

        def cross(t):
            return [
                remote(
                    pass_v.at[t, h], passed_v.at[t * SIDE + y], pass_send, pass_recv, r, LOW_X[h] * SIDE
                )
                for h in range(PER)
            ]

        def send_cross(t):
            pass_v[t] = jnp.dot(
                joined, cross_v[t].reshape(TOP * BS, BS), preferred_element_type=F32
            ).reshape(PER, LR, BS)
            for copy in cross(t):
                copy.start()

        @pl.when(y < CUT - 2 * SIDE)
        def _():
            send_cross(2)

        send_cross(1)
        send_cross(0)
        def high_block(step, k):
            slot = high_blocks_v.at[high_q]
            pl.when(y == k % SIDE)(lambda: step(k, high_mine_v.at[k - CUT], slot, True))

        for k in range(CUT, NB):
            high_block(send_block, k)
        for t in range(2):
            for copy in cross(t):
                copy.wait_send()

        @pl.when(y < CUT - 2 * SIDE)
        def _():
            for copy in cross(2):
                copy.wait_send()

        for k in range(CUT, NB):
            high_block(finish_block, k)

    @pl.when(is_low)
    def _():
        def low_block(step, k):
            step(k, low_mine_v.at[k], low_blocks_v.at[low_q], k % SIDE == 0)

        arrived(low_v, low_recv)
        arrived(low_pieces_v, part_recv)
        sums = [summed(low_pieces_v[k]) for k in range(CUT)]
        arrived(passed_v, pass_recv)
        sums = [sums[k] + passed_v[k] for k in range(CUT)]
        for j in range(CUT - 1, -1, -1):
            done = sums[j].astype(BF)
            low_mine_v[j] = done
            for k in range(j - 1, -1, -1):
                sums[k] += jnp.dot(done, low_v[tri(j) + k], preferred_element_type=F32)
        for j in range(CUT):
            low_block(send_block, j)
        for k in range(CUT):
            low_block(finish_block, k)

    @pl.when(c >= CUT)
    def _():
        arrived(high_blocks_v, block_recv)
        out_ref[0] = high_blocks_v[...].reshape(RHS, BS)

    @pl.when(c < CUT)
    def _():
        arrived(low_blocks_v, block_recv)
        out_ref[0] = low_blocks_v[...].reshape(RHS, BS)

    remote(known_v.at[rest], known_v.at[rest], known_send, known_recv, r, (c + 1) % NC).wait_send()

    @pl.when(in_top)
    def _():
        for q in range(NQ):
            finish_to(high_at(q, y), scaled_v, panel_send, top_recv)

    @pl.when(in_cross)
    def _():
        for q in range(NQ):
            finish_to(high_at(q, y), scaled_v, panel_send, cross_recv)

    @pl.when(in_low)
    def _():
        for q in range(NL):
            finish_to(low_at(q), scaled_v, panel_send, low_recv)

    @pl.when(c >= CUT)
    def _():
        for q in range(NQ):
            for i in range(SIDE):
                finish_to(high_at(q, i), high_part_v.at[q], part_send, part_recv)

    @pl.when(c < CUT)
    def _():
        for q in range(NL):
            finish_to(low_at(q), low_part_v.at[q], part_send, part_recv)


def body(rhs, diag_inv, panel, offdiag, known, row_index):
    anywhere = pl.BlockSpec(memory_space=pl.ANY)
    dma = pltpu.SemaphoreType.DMA
    regular = pltpu.SemaphoreType.REGULAR
    return pl.pallas_call(
        kernel,
        out_shape=jax.ShapeDtypeStruct((1, RHS, BS), BF),
        in_specs=[anywhere] * 5 + [pl.BlockSpec(memory_space=pltpu.SMEM)],
        out_specs=pl.BlockSpec(memory_space=pltpu.VMEM),
        scratch_shapes=[
            pltpu.VMEM((RHS, BS), F32),
            pltpu.VMEM((BS, BS), F32),
            pltpu.VMEM((BS, BS), BF),
            pltpu.VMEM((TILES, BS, BS), BF),
            pltpu.VMEM((2 * NC, RHS, BS), BF),
            pltpu.VMEM((BS, BS), BF),
            pltpu.VMEM((NQ, QR, BS), BF),
            pltpu.VMEM((NL, LR, BS), BF),
            pltpu.VMEM((TOP, NR, QR, BS), BF),
            pltpu.VMEM((CUT, NR, LR, BS), BF),
            pltpu.VMEM((tri(TOP), BS, BS), BF),
            pltpu.VMEM((3, TOP, BS, BS), BF),
            pltpu.VMEM((tri(CUT), BS, BS), BF),
            pltpu.VMEM((TOP, QR, BS), BF),
            pltpu.VMEM((CUT, LR, BS), BF),
            pltpu.VMEM((3, PER, LR, BS), F32),
            pltpu.VMEM((CUT, LR, BS), F32),
            pltpu.VMEM((NQ, QR, BS), BF),
            pltpu.VMEM((NL, LR, BS), BF),
            dma((4,)), dma, regular, regular, dma, dma,
            dma, dma, dma, dma, dma, dma,
            dma, dma, dma, dma, dma((NB,)), dma,
        ],
        compiler_params=pltpu.CompilerParams(collective_id=0, has_side_effects=True),
    )(rhs, diag_inv, panel, offdiag, known, row_index)


def solution(mesh):
    placed = (
        P("col", None, None),
        P("col", None, None),
        P("row", "col", None, None),
        P("row", "col", None, None),
        P(("row", "col"), None, None),
        P("row"),
    )
    return jax.shard_map(
        body, mesh=mesh, in_specs=placed, out_specs=P("col", None, None), check_vma=False
    )
```

```python
import jax
import jax.numpy as jnp
from jax import lax
from jax.experimental import pallas as pl
from jax.experimental.pallas import tpu as pltpu
from jax.sharding import PartitionSpec as P

NB = 16
BS = 128
RHS = 64
TILES = 64
NR = 16
NC = 16
NQ = 4
QR = RHS // NQ
NL = 8
LR = RHS // NL
PER = NL // NQ
CUT = 11
TOP = NB - CUT
SIDE = 4
MESH = pl.DeviceIdType.MESH
BF = jnp.bfloat16
F32 = jnp.float32
SPOT_Z = (2, 1, 0, 7)
HIGH_X = (3, 3, 3, 3)
LOW_X = (0, 1)


def tri(j):
    return j * (j - 1) // 2


def spot(j, k):
    d = k - CUT
    return d * (TOP - 1) - d * (d - 1) // 2 + j - k - 1


def split(value):
    high = value.astype(BF)
    return high, (value - high.astype(F32)).astype(BF)


def kernel(
    rhs_hbm, dinv_hbm, panel_hbm, offdiag_hbm, known_hbm, index_hbm, out_ref,
    rhs_v, dinv_v, panel_v, off_v, known_v, scaled_v,
    high_part_v, low_part_v, high_pieces_v, low_pieces_v, top_v, cross_v, low_v,
    high_mine_v, low_mine_v, pass_v, passed_v, high_blocks_v, low_blocks_v, row_index,
    load_sem, off_sem, planes_in, all_in, known_send, known_recv,
    panel_send, top_recv, cross_recv, low_recv, share_send, share_recv,
    part_send, part_recv, pass_send, pass_recv, block_send, block_recv,
):
    r = lax.axis_index("row")
    c = lax.axis_index("col")
    y = c % SIDE

    def signal(sem, row, col):
        pl.semaphore_signal(sem, inc=1, device_id=(row, col), device_id_type=MESH)

    def remote(src, dst, send, recv, row, col):
        return pltpu.make_async_remote_copy(
            src_ref=src, dst_ref=dst, send_sem=send, recv_sem=recv,
            device_id=(row, col), device_id_type=MESH,
        )

    def start_to(place, src, dst, send, recv):
        here = (r == place[0]) & (c == place[1])
        pl.when(here)(lambda: pltpu.make_async_copy(src, dst, recv).start())
        pl.when(jnp.logical_not(here))(lambda: remote(src, dst, send, recv, *place).start())

    def finish_to(place, src, send, recv):
        here = (r == place[0]) & (c == place[1])
        pl.when(jnp.logical_not(here))(lambda: remote(src, src, send, recv, *place).wait_send())

    def arrived(dst, sem):
        pltpu.make_async_copy(dst, dst, sem).wait()

    def high_at(q, i):
        return 2 * SPOT_Z[q], HIGH_X[q] * SIDE + i

    def low_at(g):
        return 2 * SPOT_Z[g // PER], LOW_X[g % PER] * SIDE

    def member(places):
        one, which = jnp.bool_(False), jnp.int32(0)
        for q, options in enumerate(places):
            here = jnp.bool_(False)
            for row, col in options:
                here = here | ((r == row) & (c == col))
            one, which = one | here, which + jnp.where(here, q, 0)
        return one, which

    is_high, high_q = member([[high_at(q, i) for i in range(SIDE)] for q in range(NQ)])
    is_low, low_q = member([[low_at(g)] for g in range(NL)])

    barrier = pltpu.get_barrier_semaphore()
    for d in range(1, NC):
        signal(barrier, r, (c + d) % NC)

    @pl.when(c == 0)
    def _():
        for d in range(1, NR):
            signal(barrier, (r + d) % NR, 0)

    @pl.when(is_high)
    def _():
        for j in range(CUT, NB):
            for t in range(SIDE):
                k = t * SIDE + y
                pl.when((k < j) & ((r != j) | (c != k)))(lambda: signal(barrier, j, k))

    @pl.when(is_low)
    def _():
        for j in range(1, CUT):
            for k in range(j):
                if k % SIDE == 0:
                    pl.when((r != j) | (c != k))(lambda: signal(barrier, j, k))
                else:
                    signal(barrier, j, k)

    mine = pl.ds(2 * c, 2)
    known_load = pltpu.make_async_copy(known_hbm, known_v.at[mine], load_sem.at[0])
    loads = [
        pltpu.make_async_copy(dinv_hbm.at[0], dinv_v, load_sem.at[1]),
        pltpu.make_async_copy(panel_hbm.at[0, 0], panel_v, load_sem.at[2]),
        pltpu.make_async_copy(rhs_hbm.at[0], rhs_v, load_sem.at[3]),
        pltpu.make_async_copy(index_hbm, row_index, load_sem.at[4]),
    ]
    known_load.start()
    for load in loads:
        load.start()
    off_load = pltpu.make_async_copy(offdiag_hbm.at[:, 0], off_v, off_sem)
    off_load.start()
    known_load.wait()
    greeted = NC - 1 + jnp.where(c == 0, NR - 1, 0) + jnp.where(c < r, jnp.where(r < CUT, NL, NQ), 0)
    own_target = (c < r) & jnp.where(r < CUT, is_low, is_high)
    pl.semaphore_wait(barrier, greeted - jnp.where(own_target, 1, 0))

    for d in (5, 15, 7, 13, 10, 9, 6, 14, 11, 2, 8, 1, 4, 3, 12):
        peer = ((c // SIDE + d // SIDE) % SIDE) * SIDE + (c + d) % SIDE
        remote(known_v.at[mine], known_v.at[mine], known_send, known_recv, r, peer).start()

    @pl.when(c == 0)
    def _():
        for d in range(1, NR):
            signal(planes_in, (r + d) % NR, 0)

    for load in loads:
        load.wait()
    d_high, d_low = split(dinv_v[...])
    block = panel_v[...]
    scaled = jnp.dot(
        jnp.concatenate([block, block], axis=1),
        jnp.concatenate([d_high, d_low], axis=0),
        preferred_element_type=F32,
    )
    scaled_v[...] = (-scaled).astype(BF)

    in_top = (r >= CUT) & (c >= CUT) & (c < r)
    in_cross = (r >= CUT) & (c < CUT)
    in_low = (r < CUT) & (c < r)

    def send_high_panel():
        @pl.when(in_top)
        def _():
            for q in range(NQ):
                start_to(high_at(q, y), scaled_v, top_v.at[spot(r, c)], panel_send, top_recv)

        @pl.when(in_cross)
        def _():
            for q in range(NQ):
                start_to(high_at(q, y), scaled_v, cross_v.at[c // SIDE, NB - 1 - r], panel_send, cross_recv)

    def send_low_panel():
        @pl.when(in_low)
        def _():
            for q in range(NL):
                start_to(low_at(q), scaled_v, low_v.at[tri(r) + c], panel_send, low_recv)

    send_high_panel()
    send_low_panel()

    @pl.when(c == 0)
    def _():
        pl.semaphore_wait(planes_in, NR - 1)
        for d in range(1, NC):
            signal(all_in, r, (c + d) % NC)

    @pl.when(c != 0)
    def _():
        pl.semaphore_wait(all_in, 1)

    rest = pl.ds(0, 2 * (NC - 1))
    arrived(known_v.at[rest], known_recv)
    off_load.wait()
    total = jnp.zeros((RHS, BS), F32)
    for p in range(0, TILES, 2):
        picked = jnp.concatenate([known_v[row_index[p]], known_v[row_index[p + 1]]], axis=1)
        total = total + jnp.dot(
            picked, off_v[p : p + 2].reshape(2 * BS, BS), preferred_element_type=F32
        )
    once = (r == 0).astype(F32)
    t_high, t_low = split(rhs_v[...] * once - total)
    part = jnp.dot(
        jnp.concatenate([t_high, t_high, t_low], axis=1),
        jnp.concatenate([d_high, d_low, d_high], axis=0),
        preferred_element_type=F32,
    )
    part = part.astype(BF)
    high_part_v[...] = part.reshape(NQ, QR, BS)
    low_part_v[...] = part.reshape(NL, LR, BS)

    @pl.when(c >= CUT)
    def _():
        for q in range(NQ):
            for i in range(SIDE):
                start_to(high_at(q, i), high_part_v.at[q], high_pieces_v.at[c - CUT, r], part_send, part_recv)

    @pl.when(c < CUT)
    def _():
        for q in range(NL):
            start_to(low_at(q), low_part_v.at[q], low_pieces_v.at[c, r], part_send, part_recv)

    def block_copy(k, d, block, slot):
        return remote(block, slot, block_send.at[k], block_recv, (r + d) % NR, k)

    def send_block(k, block, slot, may_be_own):
        for d in range(NR):
            if d == 0 and may_be_own:
                own = pltpu.make_async_copy(block, slot, block_recv)
                pl.when(c == k)(lambda: own.start())
                pl.when(c != k)(lambda: block_copy(k, 0, block, slot).start())
            else:
                block_copy(k, d, block, slot).start()

    def finish_block(k, block, slot, may_be_own):
        for d in range(NR):
            if d == 0 and may_be_own:
                pl.when(c != k)(lambda: block_copy(k, 0, block, slot).wait_send())
            else:
                block_copy(k, d, block, slot).wait_send()

    def summed(pieces):
        return jnp.sum(pieces.astype(F32), axis=0)

    @pl.when(is_high)
    def _():
        for k in range(CUT, NB - 1):
            count = NB - 1 - k
            column = top_v.at[pl.ds(spot(k + 1, k), count)]
            others = top_v.at[pl.ds(0, tri(TOP) - count)]

            def to(d):
                return remote(column, column, share_send, share_recv, r, c - y + (y + d) % SIDE)

            @pl.when(y == k % SIDE)
            def _():
                arrived(column, top_recv)
                for d in range(1, SIDE):
                    to(d).start()
                arrived(others, share_recv)
                for d in range(1, SIDE):
                    to(d).wait_send()

        pl.when(y < CUT - 2 * SIDE)(lambda: arrived(cross_v, cross_recv))
        pl.when(y >= CUT - 2 * SIDE)(lambda: arrived(cross_v.at[pl.ds(0, 2)], cross_recv))
        arrived(high_pieces_v, part_recv)
        sums = [summed(high_pieces_v[k]) for k in range(TOP)]
        done = [None] * TOP
        for j in range(TOP - 1, -1, -1):
            done[j] = sums[j].astype(BF)
            high_mine_v[j] = done[j]
            for k in range(j - 1, -1, -1):
                sums[k] += jnp.dot(done[j], top_v[spot(CUT + j, CUT + k)], preferred_element_type=F32)
        joined = jnp.concatenate(done[::-1], axis=1)

        def cross(t):
            return [
                remote(
                    pass_v.at[t, h], passed_v.at[t * SIDE + y], pass_send, pass_recv, r, LOW_X[h] * SIDE
                )
                for h in range(PER)
            ]

        def send_cross(t):
            pass_v[t] = jnp.dot(
                joined, cross_v[t].reshape(TOP * BS, BS), preferred_element_type=F32
            ).reshape(PER, LR, BS)
            for copy in cross(t):
                copy.start()

        @pl.when(y < CUT - 2 * SIDE)
        def _():
            send_cross(2)

        send_cross(1)
        send_cross(0)
        def high_block(step, k):
            slot = high_blocks_v.at[high_q]
            pl.when(y == k % SIDE)(lambda: step(k, high_mine_v.at[k - CUT], slot, True))

        for k in range(CUT, NB):
            high_block(send_block, k)
        for t in range(2):
            for copy in cross(t):
                copy.wait_send()

        @pl.when(y < CUT - 2 * SIDE)
        def _():
            for copy in cross(2):
                copy.wait_send()

        for k in range(CUT, NB):
            high_block(finish_block, k)

    @pl.when(is_low)
    def _():
        def low_block(step, k):
            step(k, low_mine_v.at[k], low_blocks_v.at[low_q], k % SIDE == 0)

        arrived(low_v, low_recv)
        arrived(low_pieces_v, part_recv)
        sums = [summed(low_pieces_v[k]) for k in range(CUT)]
        arrived(passed_v, pass_recv)
        sums = [sums[k] + passed_v[k] for k in range(CUT)]
        for j in range(CUT - 1, -1, -1):
            done = sums[j].astype(BF)
            low_mine_v[j] = done
            for k in range(j - 1, -1, -1):
                sums[k] += jnp.dot(done, low_v[tri(j) + k], preferred_element_type=F32)
        for j in range(CUT):
            low_block(send_block, j)
        for k in range(CUT):
            low_block(finish_block, k)

    @pl.when(c >= CUT)
    def _():
        arrived(high_blocks_v, block_recv)
        out_ref[0] = high_blocks_v[...].reshape(RHS, BS)

    @pl.when(c < CUT)
    def _():
        arrived(low_blocks_v, block_recv)
        out_ref[0] = low_blocks_v[...].reshape(RHS, BS)

    remote(known_v.at[rest], known_v.at[rest], known_send, known_recv, r, (c + 1) % NC).wait_send()

    @pl.when(in_top)
    def _():
        for q in range(NQ):
            finish_to(high_at(q, y), scaled_v, panel_send, top_recv)

    @pl.when(in_cross)
    def _():
        for q in range(NQ):
            finish_to(high_at(q, y), scaled_v, panel_send, cross_recv)

    @pl.when(in_low)
    def _():
        for q in range(NL):
            finish_to(low_at(q), scaled_v, panel_send, low_recv)

    @pl.when(c >= CUT)
    def _():
        for q in range(NQ):
            for i in range(SIDE):
                finish_to(high_at(q, i), high_part_v.at[q], part_send, part_recv)

    @pl.when(c < CUT)
    def _():
        for q in range(NL):
            finish_to(low_at(q), low_part_v.at[q], part_send, part_recv)


def body(rhs, diag_inv, panel, offdiag, known, row_index):
    operands = [
        pltpu.with_memory_space_constraint(array, pltpu.HBM)
        for array in (rhs, diag_inv, panel, offdiag, known, row_index)
    ]
    anywhere = pl.BlockSpec(memory_space=pl.ANY)
    dma = pltpu.SemaphoreType.DMA
    regular = pltpu.SemaphoreType.REGULAR
    return pl.pallas_call(
        kernel,
        out_shape=jax.ShapeDtypeStruct((1, RHS, BS), BF),
        in_specs=[anywhere] * 6,
        out_specs=pl.BlockSpec(memory_space=pltpu.VMEM),
        scratch_shapes=[
            pltpu.VMEM((RHS, BS), F32),
            pltpu.VMEM((BS, BS), F32),
            pltpu.VMEM((BS, BS), BF),
            pltpu.VMEM((TILES, BS, BS), BF),
            pltpu.VMEM((2 * NC, RHS, BS), BF),
            pltpu.VMEM((BS, BS), BF),
            pltpu.VMEM((NQ, QR, BS), BF),
            pltpu.VMEM((NL, LR, BS), BF),
            pltpu.VMEM((TOP, NR, QR, BS), BF),
            pltpu.VMEM((CUT, NR, LR, BS), BF),
            pltpu.VMEM((tri(TOP), BS, BS), BF),
            pltpu.VMEM((3, TOP, BS, BS), BF),
            pltpu.VMEM((tri(CUT), BS, BS), BF),
            pltpu.VMEM((TOP, QR, BS), BF),
            pltpu.VMEM((CUT, LR, BS), BF),
            pltpu.VMEM((3, PER, LR, BS), F32),
            pltpu.VMEM((CUT, LR, BS), F32),
            pltpu.VMEM((NQ, QR, BS), BF),
            pltpu.VMEM((NL, LR, BS), BF),
            pltpu.SMEM((TILES,), jnp.int32),
            dma((5,)), dma, regular, regular, dma, dma,
            dma, dma, dma, dma, dma, dma,
            dma, dma, dma, dma, dma((NB,)), dma,
        ],
        compiler_params=pltpu.CompilerParams(collective_id=0, has_side_effects=True, vmem_limit_bytes=24 << 20),
    )(*operands)


def solution(mesh):
    placed = (
        P("col", None, None),
        P("col", None, None),
        P("row", "col", None, None),
        P("row", "col", None, None),
        P(("row", "col"), None, None),
        P("row"),
    )
    return jax.shard_map(
        body, mesh=mesh, in_specs=placed, out_specs=P("col", None, None), check_vma=False
    )
```

```python
import jax
import jax.numpy as jnp
from jax import lax
from jax.experimental import pallas as pl
from jax.experimental.pallas import tpu as pltpu
from jax.sharding import PartitionSpec as P

NB = 16
BS = 128
RHS = 64
TILES = 64
NR = 16
NC = 16
NQ = 4
QR = RHS // NQ
NL = 8
LR = RHS // NL
PER = NL // NQ
CUT = 11
TOP = NB - CUT
SIDE = 4
MESH = pl.DeviceIdType.MESH
BF = jnp.bfloat16
F32 = jnp.float32
SPOT_Z = (2, 1, 0, 7)
HIGH_X = (3, 3, 3, 3)
LOW_X = (0, 1)


def tri(j):
    return j * (j - 1) // 2


def spot(j, k):
    d = k - CUT
    return d * (TOP - 1) - d * (d - 1) // 2 + j - k - 1


def split(value):
    high = value.astype(BF)
    return high, (value - high.astype(F32)).astype(BF)


def kernel(
    rhs_hbm, dinv_hbm, panel_hbm, offdiag_hbm, known_hbm, index_hbm, out_ref,
    rhs_v, dinv_v, panel_v, off_v, known_v, scaled_v,
    high_part_v, low_part_v, high_pieces_v, low_pieces_v, top_v, cross_v, low_v,
    high_mine_v, low_mine_v, pass_v, passed_v, high_blocks_v, low_blocks_v, row_index,
    load_sem, off_sem, planes_in, all_in, known_send, known_recv,
    panel_send, top_recv, cross_recv, low_recv, share_send, share_recv,
    part_send, part_recv, pass_send, pass_recv, block_send, block_recv,
):
    r = lax.axis_index("row")
    c = lax.axis_index("col")
    y = c % SIDE

    def signal(sem, row, col):
        pl.semaphore_signal(sem, inc=1, device_id=(row, col), device_id_type=MESH)

    def remote(src, dst, send, recv, row, col):
        return pltpu.make_async_remote_copy(
            src_ref=src, dst_ref=dst, send_sem=send, recv_sem=recv,
            device_id=(row, col), device_id_type=MESH,
        )

    def start_to(place, src, dst, send, recv):
        here = (r == place[0]) & (c == place[1])
        pl.when(here)(lambda: pltpu.make_async_copy(src, dst, recv).start())
        pl.when(jnp.logical_not(here))(lambda: remote(src, dst, send, recv, *place).start())

    def finish_to(place, src, send, recv):
        here = (r == place[0]) & (c == place[1])
        pl.when(jnp.logical_not(here))(lambda: remote(src, src, send, recv, *place).wait_send())

    def arrived(dst, sem):
        pltpu.make_async_copy(dst, dst, sem).wait()

    def high_at(q, i):
        return 2 * SPOT_Z[q], HIGH_X[q] * SIDE + i

    def low_at(g):
        return 2 * SPOT_Z[g // PER], LOW_X[g % PER] * SIDE

    def member(places):
        one, which = jnp.bool_(False), jnp.int32(0)
        for q, options in enumerate(places):
            here = jnp.bool_(False)
            for row, col in options:
                here = here | ((r == row) & (c == col))
            one, which = one | here, which + jnp.where(here, q, 0)
        return one, which

    is_high, high_q = member([[high_at(q, i) for i in range(SIDE)] for q in range(NQ)])
    is_low, low_q = member([[low_at(g)] for g in range(NL)])

    barrier = pltpu.get_barrier_semaphore()
    for d in range(1, NC):
        signal(barrier, r, (c + d) % NC)

    @pl.when(c == 0)
    def _():
        for d in range(1, NR):
            signal(barrier, (r + d) % NR, 0)

    @pl.when(is_high)
    def _():
        for j in range(CUT, NB):
            for t in range(SIDE):
                k = t * SIDE + y
                pl.when((k < j) & ((r != j) | (c != k)))(lambda: signal(barrier, j, k))

    @pl.when(is_low)
    def _():
        for j in range(1, CUT):
            for k in range(j):
                if k % SIDE == 0:
                    pl.when((r != j) | (c != k))(lambda: signal(barrier, j, k))
                else:
                    signal(barrier, j, k)

    mine = pl.ds(2 * c, 2)
    known_load = pltpu.make_async_copy(known_hbm, known_v.at[mine], load_sem.at[0])
    loads = [
        pltpu.make_async_copy(dinv_hbm.at[0], dinv_v, load_sem.at[1]),
        pltpu.make_async_copy(panel_hbm.at[0, 0], panel_v, load_sem.at[2]),
        pltpu.make_async_copy(rhs_hbm.at[0], rhs_v, load_sem.at[3]),
        pltpu.make_async_copy(index_hbm, row_index, load_sem.at[4]),
    ]
    known_load.start()
    for load in loads:
        load.start()
    off_load = pltpu.make_async_copy(offdiag_hbm.at[:, 0], off_v, off_sem)
    off_load.start()
    known_load.wait()
    greeted = NC - 1 + jnp.where(c == 0, NR - 1, 0) + jnp.where(c < r, jnp.where(r < CUT, NL, NQ), 0)
    own_target = (c < r) & jnp.where(r < CUT, is_low, is_high)
    pl.semaphore_wait(barrier, greeted - jnp.where(own_target, 1, 0))

    for d in (10, 9, 6, 14, 11, 8, 2, 5, 15, 7, 13, 1, 4, 3, 12):
        peer = ((c // SIDE + d // SIDE) % SIDE) * SIDE + (c + d) % SIDE
        remote(known_v.at[mine], known_v.at[mine], known_send, known_recv, r, peer).start()

    @pl.when(c == 0)
    def _():
        for d in range(1, NR):
            signal(planes_in, (r + d) % NR, 0)

    for load in loads:
        load.wait()
    d_high, d_low = split(dinv_v[...])
    block = panel_v[...]
    scaled = jnp.dot(
        jnp.concatenate([block, block], axis=1),
        jnp.concatenate([d_high, d_low], axis=0),
        preferred_element_type=F32,
    )
    scaled_v[...] = (-scaled).astype(BF)

    in_top = (r >= CUT) & (c >= CUT) & (c < r)
    in_cross = (r >= CUT) & (c < CUT)
    in_low = (r < CUT) & (c < r)

    def send_high_panel():
        @pl.when(in_top)
        def _():
            for q in range(NQ):
                start_to(high_at(q, y), scaled_v, top_v.at[spot(r, c)], panel_send, top_recv)

        @pl.when(in_cross)
        def _():
            for q in range(NQ):
                start_to(high_at(q, y), scaled_v, cross_v.at[c // SIDE, NB - 1 - r], panel_send, cross_recv)

    def send_low_panel():
        @pl.when(in_low)
        def _():
            for q in range(NL):
                start_to(low_at(q), scaled_v, low_v.at[tri(r) + c], panel_send, low_recv)

    send_high_panel()
    send_low_panel()

    @pl.when(c == 0)
    def _():
        pl.semaphore_wait(planes_in, NR - 1)
        for d in range(1, NC):
            signal(all_in, r, (c + d) % NC)

    @pl.when(c != 0)
    def _():
        pl.semaphore_wait(all_in, 1)

    rest = pl.ds(0, 2 * (NC - 1))
    arrived(known_v.at[rest], known_recv)
    off_load.wait()
    total = jnp.zeros((RHS, BS), F32)
    for p in range(0, TILES, 2):
        picked = jnp.concatenate([known_v[row_index[p]], known_v[row_index[p + 1]]], axis=1)
        total = total + jnp.dot(
            picked, off_v[p : p + 2].reshape(2 * BS, BS), preferred_element_type=F32
        )
    once = (r == 0).astype(F32)
    t_high, t_low = split(rhs_v[...] * once - total)
    part = jnp.dot(
        jnp.concatenate([t_high, t_high, t_low], axis=1),
        jnp.concatenate([d_high, d_low, d_high], axis=0),
        preferred_element_type=F32,
    )
    part = part.astype(BF)
    high_part_v[...] = part.reshape(NQ, QR, BS)
    low_part_v[...] = part.reshape(NL, LR, BS)

    @pl.when(c >= CUT)
    def _():
        for q in range(NQ):
            for i in range(SIDE):
                start_to(high_at(q, i), high_part_v.at[q], high_pieces_v.at[c - CUT, r], part_send, part_recv)

    @pl.when(c < CUT)
    def _():
        for q in range(NL):
            start_to(low_at(q), low_part_v.at[q], low_pieces_v.at[c, r], part_send, part_recv)

    def block_copy(k, d, block, slot):
        return remote(block, slot, block_send.at[k], block_recv, (r + d) % NR, k)

    def send_block(k, block, slot, may_be_own):
        for d in range(NR):
            if d == 0 and may_be_own:
                own = pltpu.make_async_copy(block, slot, block_recv)
                pl.when(c == k)(lambda: own.start())
                pl.when(c != k)(lambda: block_copy(k, 0, block, slot).start())
            else:
                block_copy(k, d, block, slot).start()

    def finish_block(k, block, slot, may_be_own):
        for d in range(NR):
            if d == 0 and may_be_own:
                pl.when(c != k)(lambda: block_copy(k, 0, block, slot).wait_send())
            else:
                block_copy(k, d, block, slot).wait_send()

    def summed(pieces):
        return jnp.sum(pieces.astype(F32), axis=0)

    @pl.when(is_high)
    def _():
        for k in range(CUT, NB - 1):
            count = NB - 1 - k
            column = top_v.at[pl.ds(spot(k + 1, k), count)]
            others = top_v.at[pl.ds(0, tri(TOP) - count)]

            def to(d):
                return remote(column, column, share_send, share_recv, r, c - y + (y + d) % SIDE)

            @pl.when(y == k % SIDE)
            def _():
                arrived(column, top_recv)
                for d in range(1, SIDE):
                    to(d).start()
                arrived(others, share_recv)
                for d in range(1, SIDE):
                    to(d).wait_send()

        for i in range(SIDE):
            if i not in {k % SIDE for k in range(CUT, NB - 1)}:
                pl.when(y == i)(lambda: arrived(top_v, share_recv))

        pl.when(y < CUT - 2 * SIDE)(lambda: arrived(cross_v, cross_recv))
        pl.when(y >= CUT - 2 * SIDE)(lambda: arrived(cross_v.at[pl.ds(0, 2)], cross_recv))
        arrived(high_pieces_v, part_recv)
        sums = [summed(high_pieces_v[k]) for k in range(TOP)]
        done = [None] * TOP
        for j in range(TOP - 1, -1, -1):
            done[j] = sums[j].astype(BF)
            high_mine_v[j] = done[j]
            for k in range(j - 1, -1, -1):
                sums[k] += jnp.dot(done[j], top_v[spot(CUT + j, CUT + k)], preferred_element_type=F32)
        joined = jnp.concatenate(done[::-1], axis=1)

        def cross(t):
            return [
                remote(
                    pass_v.at[t, h], passed_v.at[t * SIDE + y], pass_send, pass_recv, r, LOW_X[h] * SIDE
                )
                for h in range(PER)
            ]

        def send_cross(t):
            pass_v[t] = jnp.dot(
                joined, cross_v[t].reshape(TOP * BS, BS), preferred_element_type=F32
            ).reshape(PER, LR, BS)
            for copy in cross(t):
                copy.start()

        @pl.when(y < CUT - 2 * SIDE)
        def _():
            send_cross(2)

        send_cross(1)
        send_cross(0)
        def high_block(step, k):
            slot = high_blocks_v.at[high_q]
            pl.when(y == k % SIDE)(lambda: step(k, high_mine_v.at[k - CUT], slot, True))

        for k in range(CUT, NB):
            high_block(send_block, k)
        for t in range(2):
            for copy in cross(t):
                copy.wait_send()

        @pl.when(y < CUT - 2 * SIDE)
        def _():
            for copy in cross(2):
                copy.wait_send()

        for k in range(CUT, NB):
            high_block(finish_block, k)

    @pl.when(is_low)
    def _():
        def low_block(step, k):
            step(k, low_mine_v.at[k], low_blocks_v.at[low_q], k % SIDE == 0)

        arrived(low_v, low_recv)
        arrived(low_pieces_v, part_recv)
        sums = [summed(low_pieces_v[k]) for k in range(CUT)]
        arrived(passed_v, pass_recv)
        sums = [sums[k] + passed_v[k] for k in range(CUT)]
        for j in range(CUT - 1, -1, -1):
            done = sums[j].astype(BF)
            low_mine_v[j] = done
            for k in range(j - 1, -1, -1):
                sums[k] += jnp.dot(done, low_v[tri(j) + k], preferred_element_type=F32)
        for j in range(CUT):
            low_block(send_block, j)
        for k in range(CUT):
            low_block(finish_block, k)

    remote(known_v.at[rest], known_v.at[rest], known_send, known_recv, r, (c + 1) % NC).wait_send()

    @pl.when(in_top)
    def _():
        for q in range(NQ):
            finish_to(high_at(q, y), scaled_v, panel_send, top_recv)

    @pl.when(in_cross)
    def _():
        for q in range(NQ):
            finish_to(high_at(q, y), scaled_v, panel_send, cross_recv)

    @pl.when(in_low)
    def _():
        for q in range(NL):
            finish_to(low_at(q), scaled_v, panel_send, low_recv)

    @pl.when(c >= CUT)
    def _():
        for q in range(NQ):
            for i in range(SIDE):
                finish_to(high_at(q, i), high_part_v.at[q], part_send, part_recv)

    @pl.when(c < CUT)
    def _():
        for q in range(NL):
            finish_to(low_at(q), low_part_v.at[q], part_send, part_recv)

    @pl.when(c >= CUT)
    def _():
        arrived(high_blocks_v, block_recv)
        out_ref[0] = high_blocks_v[...].reshape(RHS, BS)

    @pl.when(c < CUT)
    def _():
        arrived(low_blocks_v, block_recv)
        out_ref[0] = low_blocks_v[...].reshape(RHS, BS)


def body(rhs, diag_inv, panel, offdiag, known, row_index):
    operands = [
        pltpu.with_memory_space_constraint(array, pltpu.HBM)
        for array in (rhs, diag_inv, panel, offdiag, known, row_index)
    ]
    anywhere = pl.BlockSpec(memory_space=pl.ANY)
    dma = pltpu.SemaphoreType.DMA
    regular = pltpu.SemaphoreType.REGULAR
    return pl.pallas_call(
        kernel,
        out_shape=jax.ShapeDtypeStruct((1, RHS, BS), BF),
        in_specs=[anywhere] * 6,
        out_specs=pl.BlockSpec(memory_space=pltpu.VMEM),
        scratch_shapes=[
            pltpu.VMEM((RHS, BS), F32),
            pltpu.VMEM((BS, BS), F32),
            pltpu.VMEM((BS, BS), BF),
            pltpu.VMEM((TILES, BS, BS), BF),
            pltpu.VMEM((2 * NC, RHS, BS), BF),
            pltpu.VMEM((BS, BS), BF),
            pltpu.VMEM((NQ, QR, BS), BF),
            pltpu.VMEM((NL, LR, BS), BF),
            pltpu.VMEM((TOP, NR, QR, BS), BF),
            pltpu.VMEM((CUT, NR, LR, BS), BF),
            pltpu.VMEM((tri(TOP), BS, BS), BF),
            pltpu.VMEM((3, TOP, BS, BS), BF),
            pltpu.VMEM((tri(CUT), BS, BS), BF),
            pltpu.VMEM((TOP, QR, BS), BF),
            pltpu.VMEM((CUT, LR, BS), BF),
            pltpu.VMEM((3, PER, LR, BS), F32),
            pltpu.VMEM((CUT, LR, BS), F32),
            pltpu.VMEM((NQ, QR, BS), BF),
            pltpu.VMEM((NL, LR, BS), BF),
            pltpu.SMEM((TILES,), jnp.int32),
            dma((5,)), dma, regular, regular, dma, dma,
            dma, dma, dma, dma, dma, dma,
            dma, dma, dma, dma, dma((NB,)), dma,
        ],
        compiler_params=pltpu.CompilerParams(collective_id=0, has_side_effects=True, vmem_limit_bytes=24 << 20),
    )(*operands)


def solution(mesh):
    placed = (
        P("col", None, None),
        P("col", None, None),
        P("row", "col", None, None),
        P("row", "col", None, None),
        P(("row", "col"), None, None),
        P("row"),
    )
    return jax.shard_map(
        body, mesh=mesh, in_specs=placed, out_specs=P("col", None, None), check_vma=False
    )
```

```python
import jax
import jax.numpy as jnp
from jax import lax
from jax.experimental import pallas as pl
from jax.experimental.pallas import tpu as pltpu
from jax.sharding import PartitionSpec as P

NB = 16
BS = 128
RHS = 64
TILES = 64
NR = 16
NC = 16
NQ = 4
QR = RHS // NQ
NL = 8
LR = RHS // NL
PER = NL // NQ
CUT = 11
TOP = NB - CUT
SIDE = 4
MESH = pl.DeviceIdType.MESH
BF = jnp.bfloat16
F32 = jnp.float32
SPOT_Z = (2, 1, 0, 7)
HIGH_X = (3, 3, 3, 3)
LOW_X = (0, 1)


def tri(j):
    return j * (j - 1) // 2


def spot(j, k):
    d = k - CUT
    return d * (TOP - 1) - d * (d - 1) // 2 + j - k - 1


def split(value):
    high = value.astype(BF)
    return high, (value - high.astype(F32)).astype(BF)


def kernel(
    rhs_hbm, dinv_hbm, panel_hbm, offdiag_hbm, known_hbm, index_hbm, out_ref,
    rhs_v, dinv_v, panel_v, off_v, known_v, scaled_v,
    high_part_v, low_part_v, high_pieces_v, low_pieces_v, top_v, cross_v, low_v,
    high_mine_v, low_mine_v, pass_v, passed_v, high_blocks_v, low_blocks_v, row_index,
    load_sem, off_sem, planes_in, all_in, known_send, known_recv,
    panel_send, top_recv, cross_recv, low_recv, share_send, share_recv,
    part_send, part_recv, pass_send, pass_recv, block_send, block_recv,
):
    r = lax.axis_index("row")
    c = lax.axis_index("col")
    y = c % SIDE

    def signal(sem, row, col):
        pl.semaphore_signal(sem, inc=1, device_id=(row, col), device_id_type=MESH)

    def remote(src, dst, send, recv, row, col):
        return pltpu.make_async_remote_copy(
            src_ref=src, dst_ref=dst, send_sem=send, recv_sem=recv,
            device_id=(row, col), device_id_type=MESH,
        )

    def start_to(place, src, dst, send, recv):
        here = (r == place[0]) & (c == place[1])
        pl.when(here)(lambda: pltpu.make_async_copy(src, dst, recv).start())
        pl.when(jnp.logical_not(here))(lambda: remote(src, dst, send, recv, *place).start())

    def finish_to(place, src, send, recv):
        here = (r == place[0]) & (c == place[1])
        pl.when(jnp.logical_not(here))(lambda: remote(src, src, send, recv, *place).wait_send())

    def arrived(dst, sem):
        pltpu.make_async_copy(dst, dst, sem).wait()

    def high_at(q, i):
        return 2 * SPOT_Z[q], HIGH_X[q] * SIDE + i

    def low_at(g):
        return 2 * SPOT_Z[g // PER], LOW_X[g % PER] * SIDE

    def member(places):
        one, which = jnp.bool_(False), jnp.int32(0)
        for q, options in enumerate(places):
            here = jnp.bool_(False)
            for row, col in options:
                here = here | ((r == row) & (c == col))
            one, which = one | here, which + jnp.where(here, q, 0)
        return one, which

    is_high, high_q = member([[high_at(q, i) for i in range(SIDE)] for q in range(NQ)])
    is_low, low_q = member([[low_at(g)] for g in range(NL)])

    barrier = pltpu.get_barrier_semaphore()
    for d in range(1, NC):
        signal(barrier, r, (c + d) % NC)

    @pl.when(c == 0)
    def _():
        for d in range(1, NR):
            signal(barrier, (r + d) % NR, 0)

    @pl.when(is_high)
    def _():
        for j in range(CUT, NB):
            for t in range(SIDE):
                k = t * SIDE + y
                pl.when((k < j) & ((r != j) | (c != k)))(lambda: signal(barrier, j, k))

    @pl.when(is_low)
    def _():
        for j in range(1, CUT):
            for k in range(j):
                if k % SIDE == 0:
                    pl.when((r != j) | (c != k))(lambda: signal(barrier, j, k))
                else:
                    signal(barrier, j, k)

    mine = pl.ds(2 * c, 2)
    known_load = pltpu.make_async_copy(known_hbm, known_v.at[mine], load_sem.at[0])
    loads = [
        pltpu.make_async_copy(dinv_hbm.at[0], dinv_v, load_sem.at[1]),
        pltpu.make_async_copy(panel_hbm.at[0, 0], panel_v, load_sem.at[2]),
        pltpu.make_async_copy(rhs_hbm.at[0], rhs_v, load_sem.at[3]),
        pltpu.make_async_copy(index_hbm, row_index, load_sem.at[4]),
    ]
    known_load.start()
    for load in loads:
        load.start()
    off_load = pltpu.make_async_copy(offdiag_hbm.at[:, 0], off_v, off_sem)
    off_load.start()
    known_load.wait()
    greeted = NC - 1 + jnp.where(c == 0, NR - 1, 0) + jnp.where(c < r, jnp.where(r < CUT, NL, NQ), 0)
    own_target = (c < r) & jnp.where(r < CUT, is_low, is_high)
    pl.semaphore_wait(barrier, greeted - jnp.where(own_target, 1, 0))

    for d in (10, 9, 6, 14, 11, 8, 2, 5, 15, 7, 13, 1, 4, 3, 12):
        peer = ((c // SIDE + d // SIDE) % SIDE) * SIDE + (c + d) % SIDE
        remote(known_v.at[mine], known_v.at[mine], known_send, known_recv, r, peer).start()

    @pl.when(c == 0)
    def _():
        for d in range(1, NR):
            signal(planes_in, (r + d) % NR, 0)

    for load in loads:
        load.wait()
    d_high, d_low = split(dinv_v[...])
    block = panel_v[...]
    scaled = jnp.dot(
        jnp.concatenate([block, block], axis=1),
        jnp.concatenate([d_high, d_low], axis=0),
        preferred_element_type=F32,
    )
    scaled_v[...] = (-scaled).astype(BF)

    in_top = (r >= CUT) & (c >= CUT) & (c < r)
    in_cross = (r >= CUT) & (c < CUT)
    in_low = (r < CUT) & (c < r)

    def send_high_panel():
        @pl.when(in_top)
        def _():
            for q in range(NQ):
                start_to(high_at(q, y), scaled_v, top_v.at[spot(r, c)], panel_send, top_recv)

        @pl.when(in_cross)
        def _():
            for q in range(NQ):
                start_to(high_at(q, y), scaled_v, cross_v.at[c // SIDE, NB - 1 - r], panel_send, cross_recv)

    def send_low_panel():
        @pl.when(in_low)
        def _():
            for q in range(NL):
                start_to(low_at(q), scaled_v, low_v.at[tri(r) + c], panel_send, low_recv)

    send_high_panel()
    send_low_panel()

    @pl.when(c == 0)
    def _():
        pl.semaphore_wait(planes_in, NR - 1)
        for d in range(1, NC):
            signal(all_in, r, (c + d) % NC)

    @pl.when(c != 0)
    def _():
        pl.semaphore_wait(all_in, 1)

    rest = pl.ds(0, 2 * (NC - 1))
    arrived(known_v.at[rest], known_recv)
    off_load.wait()
    total = jnp.zeros((RHS, BS), F32)
    for p in range(0, TILES, 2):
        picked = jnp.concatenate([known_v[row_index[p]], known_v[row_index[p + 1]]], axis=1)
        total = total + jnp.dot(
            picked, off_v[p : p + 2].reshape(2 * BS, BS), preferred_element_type=F32
        )
    once = (r == 0).astype(F32)
    t_high, t_low = split(rhs_v[...] * once - total)
    part = jnp.dot(
        jnp.concatenate([t_high, t_high, t_low], axis=1),
        jnp.concatenate([d_high, d_low, d_high], axis=0),
        preferred_element_type=F32,
    )
    part = part.astype(BF)
    high_part_v[...] = part.reshape(NQ, QR, BS)
    low_part_v[...] = part.reshape(NL, LR, BS)

    @pl.when(c >= CUT)
    def _():
        for q in (3, 0, 1, 2):
            for i in range(SIDE):
                start_to(high_at(q, i), high_part_v.at[q], high_pieces_v.at[c - CUT, r], part_send, part_recv)

    @pl.when(c < CUT)
    def _():
        for q in range(NL):
            start_to(low_at(q), low_part_v.at[q], low_pieces_v.at[c, r], part_send, part_recv)

    def block_copy(k, d, block, slot):
        return remote(block, slot, block_send.at[k], block_recv, (r + d) % NR, k)

    def send_block(k, block, slot, may_be_own):
        for d in range(NR):
            if d == 0 and may_be_own:
                own = pltpu.make_async_copy(block, slot, block_recv)
                pl.when(c == k)(lambda: own.start())
                pl.when(c != k)(lambda: block_copy(k, 0, block, slot).start())
            else:
                block_copy(k, d, block, slot).start()

    def finish_block(k, block, slot, may_be_own):
        for d in range(NR):
            if d == 0 and may_be_own:
                pl.when(c != k)(lambda: block_copy(k, 0, block, slot).wait_send())
            else:
                block_copy(k, d, block, slot).wait_send()

    def summed(pieces):
        return jnp.sum(pieces.astype(F32), axis=0)

    @pl.when(is_high)
    def _():
        for k in range(CUT, NB - 1):
            count = NB - 1 - k
            column = top_v.at[pl.ds(spot(k + 1, k), count)]
            others = top_v.at[pl.ds(0, tri(TOP) - count)]

            def to(d):
                return remote(column, column, share_send, share_recv, r, c - y + (y + d) % SIDE)

            @pl.when(y == k % SIDE)
            def _():
                arrived(column, top_recv)
                for d in range(1, SIDE):
                    to(d).start()
                arrived(others, share_recv)
                for d in range(1, SIDE):
                    to(d).wait_send()

        for i in range(SIDE):
            if i not in {k % SIDE for k in range(CUT, NB - 1)}:
                pl.when(y == i)(lambda: arrived(top_v, share_recv))

        pl.when(y < CUT - 2 * SIDE)(lambda: arrived(cross_v, cross_recv))
        pl.when(y >= CUT - 2 * SIDE)(lambda: arrived(cross_v.at[pl.ds(0, 2)], cross_recv))
        arrived(high_pieces_v, part_recv)
        sums = [summed(high_pieces_v[k]) for k in range(TOP)]
        done = [None] * TOP
        for j in range(TOP - 1, -1, -1):
            done[j] = sums[j].astype(BF)
            high_mine_v[j] = done[j]
            for k in range(j - 1, -1, -1):
                sums[k] += jnp.dot(done[j], top_v[spot(CUT + j, CUT + k)], preferred_element_type=F32)
        joined = jnp.concatenate(done[::-1], axis=1)

        def cross(t):
            return [
                remote(
                    pass_v.at[t, h], passed_v.at[t * SIDE + y], pass_send, pass_recv, r, LOW_X[h] * SIDE
                )
                for h in range(PER)
            ]

        def send_cross(t):
            pass_v[t] = jnp.dot(
                joined, cross_v[t].reshape(TOP * BS, BS), preferred_element_type=F32
            ).reshape(PER, LR, BS)
            for copy in cross(t):
                copy.start()

        @pl.when(y < CUT - 2 * SIDE)
        def _():
            send_cross(2)

        send_cross(1)
        send_cross(0)
        def high_block(step, k):
            slot = high_blocks_v.at[high_q]
            pl.when(y == k % SIDE)(lambda: step(k, high_mine_v.at[k - CUT], slot, True))

        for k in range(CUT, NB):
            high_block(send_block, k)
        for t in range(2):
            for copy in cross(t):
                copy.wait_send()

        @pl.when(y < CUT - 2 * SIDE)
        def _():
            for copy in cross(2):
                copy.wait_send()

        for k in range(CUT, NB):
            high_block(finish_block, k)

    @pl.when(is_low)
    def _():
        def low_block(step, k):
            step(k, low_mine_v.at[k], low_blocks_v.at[low_q], k % SIDE == 0)

        arrived(low_v, low_recv)
        arrived(low_pieces_v, part_recv)
        sums = [summed(low_pieces_v[k]) for k in range(CUT)]
        arrived(passed_v, pass_recv)
        sums = [sums[k] + passed_v[k] for k in range(CUT)]
        for j in range(CUT - 1, -1, -1):
            done = sums[j].astype(BF)
            low_mine_v[j] = done
            for k in range(j - 1, -1, -1):
                sums[k] += jnp.dot(done, low_v[tri(j) + k], preferred_element_type=F32)
        for rows in ((1, 0), (3, 2, 5, 4, 7, 6, 15, 14, 13, 12, 11, 10, 9, 8)):
            for k in range(CUT):
                for row in rows:
                    copy = (low_mine_v.at[k], low_blocks_v.at[low_q], block_send.at[k], block_recv)
                    if k % SIDE == 0 and row % 2 == 0:
                        start_to((row, k), *copy)
                    else:
                        remote(*copy, row, k).start()
        for k in range(CUT):
            low_block(finish_block, k)

    remote(known_v.at[rest], known_v.at[rest], known_send, known_recv, r, (c + 1) % NC).wait_send()

    @pl.when(in_top)
    def _():
        for q in range(NQ):
            finish_to(high_at(q, y), scaled_v, panel_send, top_recv)

    @pl.when(in_cross)
    def _():
        for q in range(NQ):
            finish_to(high_at(q, y), scaled_v, panel_send, cross_recv)

    @pl.when(in_low)
    def _():
        for q in range(NL):
            finish_to(low_at(q), scaled_v, panel_send, low_recv)

    @pl.when(c >= CUT)
    def _():
        for q in range(NQ):
            for i in range(SIDE):
                finish_to(high_at(q, i), high_part_v.at[q], part_send, part_recv)

    @pl.when(c < CUT)
    def _():
        for q in range(NL):
            finish_to(low_at(q), low_part_v.at[q], part_send, part_recv)

    @pl.when(c >= CUT)
    def _():
        arrived(high_blocks_v, block_recv)
        out_ref[0] = high_blocks_v[...].reshape(RHS, BS)

    @pl.when(c < CUT)
    def _():
        arrived(low_blocks_v, block_recv)
        out_ref[0] = low_blocks_v[...].reshape(RHS, BS)


def body(rhs, diag_inv, panel, offdiag, known, row_index):
    operands = [
        pltpu.with_memory_space_constraint(array, pltpu.HBM)
        for array in (rhs, diag_inv, panel, offdiag, known, row_index)
    ]
    anywhere = pl.BlockSpec(memory_space=pl.ANY)
    dma = pltpu.SemaphoreType.DMA
    regular = pltpu.SemaphoreType.REGULAR
    return pl.pallas_call(
        kernel,
        out_shape=jax.ShapeDtypeStruct((1, RHS, BS), BF),
        in_specs=[anywhere] * 6,
        out_specs=pl.BlockSpec(memory_space=pltpu.VMEM),
        scratch_shapes=[
            pltpu.VMEM((RHS, BS), F32),
            pltpu.VMEM((BS, BS), F32),
            pltpu.VMEM((BS, BS), BF),
            pltpu.VMEM((TILES, BS, BS), BF),
            pltpu.VMEM((2 * NC, RHS, BS), BF),
            pltpu.VMEM((BS, BS), BF),
            pltpu.VMEM((NQ, QR, BS), BF),
            pltpu.VMEM((NL, LR, BS), BF),
            pltpu.VMEM((TOP, NR, QR, BS), BF),
            pltpu.VMEM((CUT, NR, LR, BS), BF),
            pltpu.VMEM((tri(TOP), BS, BS), BF),
            pltpu.VMEM((3, TOP, BS, BS), BF),
            pltpu.VMEM((tri(CUT), BS, BS), BF),
            pltpu.VMEM((TOP, QR, BS), BF),
            pltpu.VMEM((CUT, LR, BS), BF),
            pltpu.VMEM((3, PER, LR, BS), F32),
            pltpu.VMEM((CUT, LR, BS), F32),
            pltpu.VMEM((NQ, QR, BS), BF),
            pltpu.VMEM((NL, LR, BS), BF),
            pltpu.SMEM((TILES,), jnp.int32),
            dma((5,)), dma, regular, regular, dma, dma,
            dma, dma, dma, dma, dma, dma,
            dma, dma, dma, dma, dma((NB,)), dma,
        ],
        compiler_params=pltpu.CompilerParams(collective_id=0, has_side_effects=True, vmem_limit_bytes=24 << 20),
    )(*operands)


def solution(mesh):
    placed = (
        P("col", None, None),
        P("col", None, None),
        P("row", "col", None, None),
        P("row", "col", None, None),
        P(("row", "col"), None, None),
        P("row"),
    )
    return jax.shard_map(
        body, mesh=mesh, in_specs=placed, out_specs=P("col", None, None), check_vma=False
    )
```

```python
import jax
import jax.numpy as jnp
from jax import lax
from jax.experimental import pallas as pl
from jax.experimental.pallas import tpu as pltpu
from jax.sharding import PartitionSpec as P

NB = 16
BS = 128
RHS = 64
TILES = 64
NR = 16
NC = 16
NQ = 4
QR = RHS // NQ
NL = 8
LR = RHS // NL
PER = NL // NQ
CUT = 11
TOP = NB - CUT
SIDE = 4
MESH = pl.DeviceIdType.MESH
BF = jnp.bfloat16
F32 = jnp.float32
SPOT_Z = (2, 1, 0, 7)
HIGH_X = (3, 3, 3, 3)
LOW_X = (0, 1)


def tri(j):
    return j * (j - 1) // 2


def spot(j, k):
    d = k - CUT
    return d * (TOP - 1) - d * (d - 1) // 2 + j - k - 1


def split(value):
    high = value.astype(BF)
    return high, (value - high.astype(F32)).astype(BF)


def kernel(
    rhs_hbm, dinv_hbm, panel_hbm, offdiag_hbm, known_hbm, index_hbm, out_ref,
    rhs_v, dinv_v, panel_v, off_v, known_v, scaled_v,
    high_part_v, low_part_v, high_pieces_v, low_pieces_v, top_v, cross_v, low_v,
    high_mine_v, low_mine_v, pass_v, passed_v, high_blocks_v, low_blocks_v, row_index,
    load_sem, off_sem, planes_in, all_in, known_send, known_recv,
    panel_send, top_recv, cross_recv, low_recv, share_send, share_recv,
    part_send, part_recv, pass_send, pass_recv, block_send, block_recv,
):
    r = lax.axis_index("row")
    c = lax.axis_index("col")
    y = c % SIDE

    def signal(sem, row, col):
        pl.semaphore_signal(sem, inc=1, device_id=(row, col), device_id_type=MESH)

    def remote(src, dst, send, recv, row, col):
        return pltpu.make_async_remote_copy(
            src_ref=src, dst_ref=dst, send_sem=send, recv_sem=recv,
            device_id=(row, col), device_id_type=MESH,
        )

    def start_to(place, src, dst, send, recv):
        here = (r == place[0]) & (c == place[1])
        pl.when(here)(lambda: pltpu.make_async_copy(src, dst, recv).start())
        pl.when(jnp.logical_not(here))(lambda: remote(src, dst, send, recv, *place).start())

    def finish_to(place, src, send, recv):
        here = (r == place[0]) & (c == place[1])
        pl.when(jnp.logical_not(here))(lambda: remote(src, src, send, recv, *place).wait_send())

    def arrived(dst, sem):
        pltpu.make_async_copy(dst, dst, sem).wait()

    def high_at(q, i):
        return 2 * SPOT_Z[q], HIGH_X[q] * SIDE + i

    def low_at(g):
        return 2 * SPOT_Z[g // PER], LOW_X[g % PER] * SIDE

    def member(places):
        one, which = jnp.bool_(False), jnp.int32(0)
        for q, options in enumerate(places):
            here = jnp.bool_(False)
            for row, col in options:
                here = here | ((r == row) & (c == col))
            one, which = one | here, which + jnp.where(here, q, 0)
        return one, which

    is_high, high_q = member([[high_at(q, i) for i in range(SIDE)] for q in range(NQ)])
    is_low, low_q = member([[low_at(g)] for g in range(NL)])

    barrier = pltpu.get_barrier_semaphore()
    for d in range(1, NC):
        signal(barrier, r, (c + d) % NC)

    @pl.when(c == 0)
    def _():
        for d in range(1, NR):
            signal(barrier, (r + d) % NR, 0)

    @pl.when(is_high)
    def _():
        for j in range(CUT, NB):
            for t in range(SIDE):
                k = t * SIDE + y
                pl.when((k < j) & ((r != j) | (c != k)))(lambda: signal(barrier, j, k))

    @pl.when(is_low)
    def _():
        for j in range(1, CUT):
            for k in range(j):
                if k % SIDE == 0:
                    pl.when((r != j) | (c != k))(lambda: signal(barrier, j, k))
                else:
                    signal(barrier, j, k)

    mine = pl.ds(2 * c, 2)
    known_load = pltpu.make_async_copy(known_hbm, known_v.at[mine], load_sem.at[0])
    loads = [
        pltpu.make_async_copy(dinv_hbm.at[0], dinv_v, load_sem.at[1]),
        pltpu.make_async_copy(panel_hbm.at[0, 0], panel_v, load_sem.at[2]),
        pltpu.make_async_copy(rhs_hbm.at[0], rhs_v, load_sem.at[3]),
        pltpu.make_async_copy(index_hbm, row_index, load_sem.at[4]),
    ]
    known_load.start()
    for load in loads:
        load.start()
    off_load = pltpu.make_async_copy(offdiag_hbm.at[:, 0], off_v, off_sem)
    off_load.start()
    greeted = NC - 1 + jnp.where(c == 0, NR - 1, 0) + jnp.where(c < r, jnp.where(r < CUT, NL, NQ), 0)
    own_target = (c < r) & jnp.where(r < CUT, is_low, is_high)
    pl.semaphore_wait(barrier, greeted - jnp.where(own_target, 1, 0))

    for d in (10, 9, 6, 14, 11, 8, 2, 5, 15, 7, 13, 1, 4, 3, 12):
        peer = ((c // SIDE + d // SIDE) % SIDE) * SIDE + (c + d) % SIDE
        remote(known_hbm, known_v.at[mine], known_send, known_recv, r, peer).start()

    @pl.when(c == 0)
    def _():
        for d in range(1, NR):
            signal(planes_in, (r + d) % NR, 0)

    for load in loads:
        load.wait()
    d_high, d_low = split(dinv_v[...])
    block = panel_v[...]
    scaled = jnp.dot(
        jnp.concatenate([block, block], axis=1),
        jnp.concatenate([d_high, d_low], axis=0),
        preferred_element_type=F32,
    )
    scaled_v[...] = (-scaled).astype(BF)

    in_top = (r >= CUT) & (c >= CUT) & (c < r)
    in_cross = (r >= CUT) & (c < CUT)
    in_low = (r < CUT) & (c < r)

    def send_high_panel():
        @pl.when(in_top)
        def _():
            for q in range(NQ):
                start_to(high_at(q, y), scaled_v, top_v.at[spot(r, c)], panel_send, top_recv)

        @pl.when(in_cross)
        def _():
            for q in range(NQ):
                start_to(high_at(q, y), scaled_v, cross_v.at[c // SIDE, NB - 1 - r], panel_send, cross_recv)

    def send_low_panel():
        @pl.when(in_low)
        def _():
            for q in range(NL):
                start_to(low_at(q), scaled_v, low_v.at[tri(r) + c], panel_send, low_recv)

    send_high_panel()
    send_low_panel()

    @pl.when(c == 0)
    def _():
        pl.semaphore_wait(planes_in, NR - 1)
        for d in range(1, NC):
            signal(all_in, r, (c + d) % NC)

    @pl.when(c != 0)
    def _():
        pl.semaphore_wait(all_in, 1)

    rest = pl.ds(0, 2 * (NC - 1))
    known_load.wait()
    arrived(known_v.at[rest], known_recv)
    off_load.wait()
    total = jnp.zeros((RHS, BS), F32)
    for p in range(0, TILES, 2):
        picked = jnp.concatenate([known_v[row_index[p]], known_v[row_index[p + 1]]], axis=1)
        total = total + jnp.dot(
            picked, off_v[p : p + 2].reshape(2 * BS, BS), preferred_element_type=F32
        )
    once = (r == 0).astype(F32)
    t_high, t_low = split(rhs_v[...] * once - total)
    part = jnp.dot(
        jnp.concatenate([t_high, t_high, t_low], axis=1),
        jnp.concatenate([d_high, d_low, d_high], axis=0),
        preferred_element_type=F32,
    )
    part = part.astype(BF)
    high_part_v[...] = part.reshape(NQ, QR, BS)
    low_part_v[...] = part.reshape(NL, LR, BS)

    @pl.when(c >= CUT)
    def _():
        for q in (3, 0, 1, 2):
            for i in range(SIDE):
                start_to(high_at(q, i), high_part_v.at[q], high_pieces_v.at[c - CUT, r], part_send, part_recv)

    @pl.when(c < CUT)
    def _():
        for q in range(NL):
            start_to(low_at(q), low_part_v.at[q], low_pieces_v.at[c, r], part_send, part_recv)

    def block_copy(k, d, block, slot):
        return remote(block, slot, block_send.at[k], block_recv, (r + d) % NR, k)

    def send_block(k, block, slot, may_be_own):
        for d in range(NR):
            if d == 0 and may_be_own:
                own = pltpu.make_async_copy(block, slot, block_recv)
                pl.when(c == k)(lambda: own.start())
                pl.when(c != k)(lambda: block_copy(k, 0, block, slot).start())
            else:
                block_copy(k, d, block, slot).start()

    def finish_block(k, block, slot, may_be_own):
        for d in range(NR):
            if d == 0 and may_be_own:
                pl.when(c != k)(lambda: block_copy(k, 0, block, slot).wait_send())
            else:
                block_copy(k, d, block, slot).wait_send()

    def summed(pieces):
        return jnp.sum(pieces.astype(F32), axis=0)

    @pl.when(is_high)
    def _():
        for k in range(CUT, NB - 1):
            count = NB - 1 - k
            column = top_v.at[pl.ds(spot(k + 1, k), count)]
            others = top_v.at[pl.ds(0, tri(TOP) - count)]

            def to(d):
                return remote(column, column, share_send, share_recv, r, c - y + (y + d) % SIDE)

            @pl.when(y == k % SIDE)
            def _():
                arrived(column, top_recv)
                for d in range(1, SIDE):
                    to(d).start()
                arrived(others, share_recv)
                for d in range(1, SIDE):
                    to(d).wait_send()

        for i in range(SIDE):
            if i not in {k % SIDE for k in range(CUT, NB - 1)}:
                pl.when(y == i)(lambda: arrived(top_v, share_recv))

        pl.when(y < CUT - 2 * SIDE)(lambda: arrived(cross_v, cross_recv))
        pl.when(y >= CUT - 2 * SIDE)(lambda: arrived(cross_v.at[pl.ds(0, 2)], cross_recv))
        arrived(high_pieces_v, part_recv)
        sums = [summed(high_pieces_v[k]) for k in range(TOP)]
        done = [None] * TOP
        for j in range(TOP - 1, -1, -1):
            done[j] = sums[j].astype(BF)
            high_mine_v[j] = done[j]
            for k in range(j - 1, -1, -1):
                sums[k] += jnp.dot(done[j], top_v[spot(CUT + j, CUT + k)], preferred_element_type=F32)
        joined = jnp.concatenate(done[::-1], axis=1)

        def cross(t):
            return [
                remote(
                    pass_v.at[t, h], passed_v.at[t * SIDE + y], pass_send, pass_recv, r, LOW_X[h] * SIDE
                )
                for h in range(PER)
            ]

        def send_cross(t):
            pass_v[t] = jnp.dot(
                joined, cross_v[t].reshape(TOP * BS, BS), preferred_element_type=F32
            ).reshape(PER, LR, BS)
            for copy in cross(t):
                copy.start()

        @pl.when(y < CUT - 2 * SIDE)
        def _():
            send_cross(2)

        send_cross(1)
        send_cross(0)
        def high_block(step, k):
            slot = high_blocks_v.at[high_q]
            pl.when(y == k % SIDE)(lambda: step(k, high_mine_v.at[k - CUT], slot, True))

        for k in range(CUT, NB):
            high_block(send_block, k)
        for t in range(2):
            for copy in cross(t):
                copy.wait_send()

        @pl.when(y < CUT - 2 * SIDE)
        def _():
            for copy in cross(2):
                copy.wait_send()

        for k in range(CUT, NB):
            high_block(finish_block, k)

    @pl.when(is_low)
    def _():
        def low_block(step, k):
            step(k, low_mine_v.at[k], low_blocks_v.at[low_q], k % SIDE == 0)

        arrived(low_v, low_recv)
        arrived(low_pieces_v, part_recv)
        sums = [summed(low_pieces_v[k]) for k in range(CUT)]
        arrived(passed_v, pass_recv)
        sums = [sums[k] + passed_v[k] for k in range(CUT)]
        for j in range(CUT - 1, -1, -1):
            done = sums[j].astype(BF)
            low_mine_v[j] = done
            for k in range(j - 1, -1, -1):
                sums[k] += jnp.dot(done, low_v[tri(j) + k], preferred_element_type=F32)
        for rows in ((1, 0), (3, 2, 5, 4, 7, 6, 15, 14, 13, 12, 11, 10, 9, 8)):
            for k in range(CUT):
                for row in rows:
                    copy = (low_mine_v.at[k], low_blocks_v.at[low_q], block_send.at[k], block_recv)
                    if k % SIDE == 0 and row % 2 == 0:
                        start_to((row, k), *copy)
                    else:
                        remote(*copy, row, k).start()
        for k in range(CUT):
            low_block(finish_block, k)

    remote(known_v.at[rest], known_v.at[rest], known_send, known_recv, r, (c + 1) % NC).wait_send()

    @pl.when(in_top)
    def _():
        for q in range(NQ):
            finish_to(high_at(q, y), scaled_v, panel_send, top_recv)

    @pl.when(in_cross)
    def _():
        for q in range(NQ):
            finish_to(high_at(q, y), scaled_v, panel_send, cross_recv)

    @pl.when(in_low)
    def _():
        for q in range(NL):
            finish_to(low_at(q), scaled_v, panel_send, low_recv)

    @pl.when(c >= CUT)
    def _():
        for q in range(NQ):
            for i in range(SIDE):
                finish_to(high_at(q, i), high_part_v.at[q], part_send, part_recv)

    @pl.when(c < CUT)
    def _():
        for q in range(NL):
            finish_to(low_at(q), low_part_v.at[q], part_send, part_recv)

    @pl.when(c >= CUT)
    def _():
        arrived(high_blocks_v, block_recv)
        out_ref[0] = high_blocks_v[...].reshape(RHS, BS)

    @pl.when(c < CUT)
    def _():
        arrived(low_blocks_v, block_recv)
        out_ref[0] = low_blocks_v[...].reshape(RHS, BS)


def body(rhs, diag_inv, panel, offdiag, known, row_index):
    operands = [
        pltpu.with_memory_space_constraint(array, pltpu.HBM)
        for array in (rhs, diag_inv, panel, offdiag, known, row_index)
    ]
    anywhere = pl.BlockSpec(memory_space=pl.ANY)
    dma = pltpu.SemaphoreType.DMA
    regular = pltpu.SemaphoreType.REGULAR
    return pl.pallas_call(
        kernel,
        out_shape=jax.ShapeDtypeStruct((1, RHS, BS), BF),
        in_specs=[anywhere] * 6,
        out_specs=pl.BlockSpec(memory_space=pltpu.VMEM),
        scratch_shapes=[
            pltpu.VMEM((RHS, BS), F32),
            pltpu.VMEM((BS, BS), F32),
            pltpu.VMEM((BS, BS), BF),
            pltpu.VMEM((TILES, BS, BS), BF),
            pltpu.VMEM((2 * NC, RHS, BS), BF),
            pltpu.VMEM((BS, BS), BF),
            pltpu.VMEM((NQ, QR, BS), BF),
            pltpu.VMEM((NL, LR, BS), BF),
            pltpu.VMEM((TOP, NR, QR, BS), BF),
            pltpu.VMEM((CUT, NR, LR, BS), BF),
            pltpu.VMEM((tri(TOP), BS, BS), BF),
            pltpu.VMEM((3, TOP, BS, BS), BF),
            pltpu.VMEM((tri(CUT), BS, BS), BF),
            pltpu.VMEM((TOP, QR, BS), BF),
            pltpu.VMEM((CUT, LR, BS), BF),
            pltpu.VMEM((3, PER, LR, BS), F32),
            pltpu.VMEM((CUT, LR, BS), F32),
            pltpu.VMEM((NQ, QR, BS), BF),
            pltpu.VMEM((NL, LR, BS), BF),
            pltpu.SMEM((TILES,), jnp.int32),
            dma((5,)), dma, regular, regular, dma, dma,
            dma, dma, dma, dma, dma, dma,
            dma, dma, dma, dma, dma((NB,)), dma,
        ],
        compiler_params=pltpu.CompilerParams(collective_id=0, has_side_effects=True, vmem_limit_bytes=24 << 20),
    )(*operands)


def solution(mesh):
    placed = (
        P("col", None, None),
        P("col", None, None),
        P("row", "col", None, None),
        P("row", "col", None, None),
        P(("row", "col"), None, None),
        P("row"),
    )
    return jax.shard_map(
        body, mesh=mesh, in_specs=placed, out_specs=P("col", None, None), check_vma=False
    )
```
